512 devices in a mesh: item: 8 (over y), rows: 32 (over z, x_hi, core), hid: 2 (over x_lo).
Axes of the slice: x: 4 (x_hi: 2, x_lo: 2; x = x_hi * 2 + x_lo), y: 8, z: 8, core: 2. Of those that a mesh axis runs over, the one named last changes fastest.
Arguments:
- latents: float32 [16, 32, 2048], P('item', 'rows'), may hold values from -6 to 6
- heights: int32 [16], P('item'), may hold values from 8 to 32, as said below
- widths: int32 [16], P('item'), may hold values from 8 to 32, as said below
- slot_item: int32 [16], P('item'), may hold values from 0 to 15, each once
- step_index: int32 [1], replicated, may hold values from 0 to 27
- cond_table: float32 [16, 5, 1536], replicated, may hold values from -9 to 9
- text_kv: bfloat16 [16, 2, 154, 768], P('item', None, None, 'hid'), may hold values from -175 to 175
- patch_weight: bfloat16 [64, 1536], replicated, may hold values from -0.75 to 0.75
- qkv_weight: bfloat16 [3, 1536, 768], P(None, ('item', 'rows'), 'hid'), may hold values from -0.15625 to 0.15625
- out_weight: bfloat16 [768, 1536], P('hid', ('item', 'rows')), may hold values from -0.21875 to 0.21875
- final_weight: bfloat16 [1536, 64], replicated, may hold values from -0.15625 to 0.15625
Outputs:
- next_latents: float32 [16, 32, 2048], P('item', 'rows')
- denoised: float32 [16, 32, 2048], P('item', 'rows')
The draws below stay inside these ranges and needn't reach their ends.
Inputs may be any that keep to these rules, and one draw needn't show every extreme that they name: `heights`: every grid has at least 8 rows, and some item has exactly 32. `widths`: every grid has at least 8 columns, and some item has exactly 32. `slot_item`: each request is served by exactly one slot.
All inputs are finite; a program needn't handle non-finite values.
Results may differ from the reference program's by a relative error of at most 0.007.
Values may be sent and summed in bfloat16 or wider, within the bound.
A program may use at most 64 MiB of HBM per device.

```python
import jax
import jax.numpy as jnp
from jax import lax

D = 1536
HD = 64
CH = 64
HEADS = 12
TXT = 154
PW = 32
STEPS = 28
HW = 768
PH = 32
ITEMS = 16


def grid_extent(key, largest):
    lowest = max(1, largest // 4)
    values = jax.random.randint(key, (ITEMS,), lowest, largest + 1)
    chosen = jax.random.randint(jax.random.fold_in(key, 7), (), 0, ITEMS)
    return jnp.where(jnp.arange(ITEMS) == chosen, largest, values).astype(jnp.int32)


def draw_heights(key, part):
    return grid_extent(jax.random.fold_in(key, 1), PH)


def draw_widths(key, part):
    return grid_extent(jax.random.fold_in(key, 2), PW)


def draw_cond_table(key, part):
    base = jnp.clip(0.5 * jax.random.normal(jax.random.fold_in(key, 11), (ITEMS, 5, D), jnp.float32), -3.0, 3.0)
    gate_rows = jnp.clip(3.0 * jax.random.normal(jax.random.fold_in(key, 12), (ITEMS, 1, D), jnp.float32), -9.0, 9.0)
    return jnp.concatenate([base[:, 0:2], gate_rows, base[:, 3:5]], 1)


def draw_text_kv(key, part):
    full_shape = (ITEMS, 2, TXT, HW)
    values = jnp.clip(jax.random.normal(key, full_shape, jnp.float32), -4.0, 4.0)
    return values.astype(jnp.bfloat16)


def shard_levels(key, shape, split, smallest, high):
    gain = 1.0
    for dim, shards_of in split:
        steps = jax.random.uniform(jax.random.fold_in(jax.random.fold_in(key, 6), dim), (shards_of,), jnp.float32, smallest / len(split), high / len(split))
        gain = gain * jnp.repeat(jnp.exp(steps), shape[dim] // shards_of).reshape((-1,) + (1,) * (len(shape) - 1 - dim))
    return gain


def gaussian(key, dims, scale, bound, pieces=(), held_as=jnp.bfloat16):
    loudness = shard_levels(key, dims, pieces, -0.22, 0.18) if pieces else 1.0
    array = jax.random.normal(key, dims, jnp.float32) * scale * loudness
    return jnp.minimum(jnp.maximum(array, -bound), bound).astype(held_as)


def setup_inputs(seed: int = 0) -> dict:
    streams_of = jax.random.split(jax.random.key(seed), 12)
    latents = gaussian(streams_of[0], (ITEMS, PH, PW * CH), 1.0, 6.0, ((0, 8), (1, 32)), jnp.float32)
    heights = draw_heights(jax.random.fold_in(streams_of[11], 71), 0)
    widths = draw_widths(jax.random.fold_in(streams_of[11], 71), 0)
    slot_item = jax.random.permutation(streams_of[3], ITEMS).astype(jnp.int32)
    step_index = jax.random.randint(streams_of[4], (1,), 0, STEPS).astype(jnp.int32)
    cond_table = draw_cond_table(jax.random.fold_in(streams_of[11], 71), 0)
    text_kv = draw_text_kv(jax.random.fold_in(streams_of[11], 71), 0)
    patch_weight = gaussian(streams_of[7], (CH, D), CH ** -0.5, 0.75)
    qkv_weight = gaussian(streams_of[8], (3, D, HW), D ** -0.5, 0.15625, ((1, 256), (2, 2)))
    out_weight = gaussian(streams_of[9], (HW, D), HW ** -0.5, 0.21875, ((0, 2), (1, 256)))
    final_weight = gaussian(streams_of[10], (D, CH), D ** -0.5, 0.15625)
    return dict(latents=latents, heights=heights, widths=widths, slot_item=slot_item, step_index=step_index, cond_table=cond_table, text_kv=text_kv, patch_weight=patch_weight, qkv_weight=qkv_weight, out_weight=out_weight, final_weight=final_weight)


def sigma_level(position):
    fraction = 1.0 - position / STEPS
    return 3.0 * fraction / (1.0 + 2.0 * fraction)

def position_embed(row_pos, col_count, model_width):
    quarter = model_width // 4
    frequency = 1.0 / 10000.0 ** (jnp.arange(quarter, dtype=jnp.float32) / quarter)
    col_pos = jnp.arange(col_count, dtype=jnp.float32)
    row_angle = row_pos[:, None] * frequency[None, :]
    col_angle = col_pos[:, None] * frequency[None, :]
    row_part = jnp.concatenate([jnp.sin(row_angle), jnp.cos(row_angle)], 1)
    col_part = jnp.concatenate([jnp.sin(col_angle), jnp.cos(col_angle)], 1)
    row_full = jnp.broadcast_to(row_part[:, None, :], (row_pos.shape[0], col_count, model_width // 2))
    col_full = jnp.broadcast_to(col_part[None, :, :], (row_pos.shape[0], col_count, model_width // 2))
    return jnp.concatenate([row_full, col_full], 2)

def normalize(values):
    mean_rows = lax.optimization_barrier(jnp.mean(values, -1, keepdims=True))
    centered = values - mean_rows
    return centered * lax.rsqrt(lax.optimization_barrier(jnp.mean(centered * centered, -1, keepdims=True)) + 1e-06)

def reference(latents, heights, widths, slot_item, step_index, cond_table, text_kv, patch_weight, qkv_weight, out_weight, final_weight):
    places = position_embed(jnp.arange(PH, dtype=jnp.float32), PW, D).reshape(PH * PW, D)
    row_index = jnp.arange(PH, dtype=jnp.int32)
    col_index = jnp.arange(PW, dtype=jnp.int32)
    position = step_index[0].astype(jnp.float32)
    sigma_now = sigma_level(position)
    sigma_next = sigma_level(position + 1.0)

    def one_item(packed):
        latent_item, height, width_item, entry_id, text_pair = packed
        conditions = lax.dynamic_index_in_dim(cond_table, entry_id, 0, keepdims=False)
        patches = latent_item.reshape(PH * PW, CH).astype(jnp.bfloat16)
        embedded = jnp.dot(patches, patch_weight, preferred_element_type=jnp.float32) + places
        normed = (normalize(embedded) * (1.0 + conditions[1]) + conditions[0]).astype(jnp.bfloat16)
        queries = jnp.dot(normed, qkv_weight[0], preferred_element_type=jnp.float32).astype(jnp.bfloat16)
        key_rows = jnp.dot(normed, qkv_weight[1], preferred_element_type=jnp.float32).astype(jnp.bfloat16)
        val_rows = jnp.dot(normed, qkv_weight[2], preferred_element_type=jnp.float32).astype(jnp.bfloat16)
        live_mask = ((row_index[:, None] < height) & (col_index[None, :] < width_item)).reshape(PH * PW)
        all_keys = lax.optimization_barrier(jnp.concatenate([text_pair[0], key_rows], 0)).astype(jnp.float32)
        all_vals = lax.optimization_barrier(jnp.concatenate([text_pair[1], val_rows], 0)).astype(jnp.float32)
        all_keys = all_keys.reshape(TXT + PH * PW, HEADS, HD)
        all_vals = all_vals.reshape(TXT + PH * PW, HEADS, HD)
        valid_keys = jnp.concatenate([jnp.ones((TXT,), dtype=bool), live_mask], 0)
        query_f = lax.optimization_barrier(queries).astype(jnp.float32).reshape(PH * PW, HEADS, HD)
        scores = jnp.einsum('qhd,khd->hqk', query_f, all_keys) * HD ** (-0.5)
        scores = jnp.where(valid_keys[None, None, :], scores, -1e+30)
        run_top = lax.optimization_barrier(jnp.max(scores, -1, keepdims=True))
        weights = jnp.exp(scores - run_top)
        run_total = lax.optimization_barrier(jnp.sum(weights, -1))
        rounded = lax.optimization_barrier(weights.astype(jnp.bfloat16)).astype(jnp.float32)
        run_acc = jnp.einsum('hqk,khd->hqd', rounded, all_vals)
        attended = (run_acc / run_total[..., None]).transpose(1, 0, 2).reshape(PH * PW, HW).astype(jnp.bfloat16)
        projected = jnp.dot(attended, out_weight, preferred_element_type=jnp.float32)
        residual = embedded + conditions[2] * projected
        final_in = (normalize(residual) * (1.0 + conditions[4]) + conditions[3]).astype(jnp.bfloat16)
        velocity = jnp.dot(final_in, final_weight, preferred_element_type=jnp.float32)
        live_velocity = jnp.where(live_mask[:, None], velocity, 0.0).reshape(PH, PW * CH)
        return (latent_item + (sigma_next - sigma_now) * live_velocity, latent_item - sigma_now * live_velocity)
    next_latents, denoised = lax.map(one_item, (latents, heights, widths, slot_item, text_kv))
    return (next_latents, denoised)
```

```python
import functools

import jax
import jax.numpy as jnp
import numpy as np
from jax import lax
from jax.experimental import pallas as pl
from jax.experimental.pallas import tpu as pltpu
from jax.sharding import PartitionSpec as P

MESH = pl.DeviceIdType.MESH
HD = 64
STEPS = 28
D = 1536
NY, NZ = 8, 8
UR = 96
F32, BF16 = jnp.float32, jnp.bfloat16


def feature_order():
    order = np.zeros((D,), np.int32)
    at = 0
    for core in range(2):
        for outer in range(8):
            for inner in range(8):
                y, z = (outer, inner) if core == 0 else (inner, outer)
                for xh in range(2):
                    block = y * 32 + z * 4 + xh * 2 + core
                    order[at : at + 6] = 6 * block + np.arange(6)
                    at += 6
    return order


def tables():
    order = feature_order()
    quarter = D // 4
    frequency = (
        np.float32(1.0) / np.float32(10000.0) ** (np.arange(quarter, dtype=np.float32) / np.float32(quarter))
    ).astype(np.float32)
    angle = np.arange(32, dtype=np.float32)[:, None] * frequency[None, :]
    part = np.concatenate([np.sin(angle.astype(np.float64)), np.cos(angle.astype(np.float64))], 1)
    zero = np.zeros_like(part)
    row_table = np.concatenate([part, zero], 1)[:, order].astype(np.float32)
    col_table = np.concatenate([zero, part], 1)[:, order].astype(np.float32)
    pick = np.zeros((480, 1), np.int32)
    for tile in range(5):
        for source in range(16):
            for j in range(6):
                pick[tile * 96 + source * 6 + j, 0] = source * 32 + tile * 6 + j
    col_table = np.stack([col_table[0::2], col_table[1::2]])
    return order[None, :], pick, row_table[:, None, :], col_table


def relative_partners():
    found = set()
    for dy in range(NY):
        for dz in range(NZ):
            for dxh in range(2):
                for dc in range(2):
                    for dxl in range(2):
                        near = (dy == 0 and dxl == 0) or (dy == 0 and dz == 0)
                        near = near or (dc == 0 and (dy == 0 or dz == 0))
                        if near:
                            found.add((dy, dz, dxh, dc, dxl))
    found.discard((0, 0, 0, 0, 0))
    return sorted(found)


def kernel(
    heights,
    widths,
    slot_item,
    step_index,
    lat,
    latb,
    cond,
    text,
    wp,
    wft,
    qpiece,
    opiece,
    order,
    pick,
    rowtab,
    coltab,
    next_out,
    den_out,
    lb,
    qb,
    ob,
    qu,
    ou,
    nb,
    kvb,
    wps,
    wfs,
    cperm,
    rows_in,
    rows_out,
    eb,
    send_att,
    recv_att,
    sem_ls,
    sem_lr,
    sem_qs,
    sem_qr,
    sem_os,
    sem_or,
    sem_us,
    sem_ur,
    sem_ps,
    sem_pr,
    sem_ws,
    sem_wr,
    sem_xs,
    sem_xr,
    sem_as,
    sem_ar,
):
    y = lax.axis_index("item")
    rows = lax.axis_index("rows")
    xl = lax.axis_index("hid")
    z = rows // 4
    xh = (rows // 2) % 2
    core = rows % 2
    by_b = z * (1 - core) + y * core
    by_c = y * (1 - core) + z * core

    def flip(bit, change):
        return bit if change == 0 else 1 - bit

    def device(ty, tz, txh, tc, txl):
        return (ty, tz * 4 + txh * 2 + tc, txl)

    def ring_b(k):
        return (y + core * k) % 8, (z + (1 - core) * k) % 8

    def ring_c(k):
        return (y + (1 - core) * k) % 8, (z + core * k) % 8

    barrier = pltpu.get_barrier_semaphore()
    partners = relative_partners()
    for dy, dz, dxh, dc, dxl in partners:
        pl.semaphore_signal(
            barrier,
            inc=1,
            device_id=device((y + dy) % 8, (z + dz) % 8, flip(xh, dxh), flip(core, dc), flip(xl, dxl)),
            device_id_type=MESH,
        )
    lb[rows] = latb[core]
    qb[by_b * 2 + xh] = qpiece[xh]
    ob[xl * 16 + by_b * 2 + xh] = opiece[...]
    pl.semaphore_wait(barrier, len(partners))

    def remote(src, dst, s_sem, r_sem, to):
        return pltpu.make_async_remote_copy(
            src_ref=src, dst_ref=dst, send_sem=s_sem, recv_sem=r_sem, device_id=to, device_id_type=MESH
        )

    q_copies, l_copies, o_copies = [], [], []
    for k in range(8):
        for dxh in range(2):
            if k == 0 and dxh == 0:
                continue
            ty, tz = ring_b(k)
            txh = flip(xh, dxh)
            n = k * 2 + dxh
            q_copies.append(
                remote(
                    qpiece.at[txh],
                    qb.at[by_b * 2 + xh],
                    sem_qs.at[n],
                    sem_qr.at[n],
                    device(ty, tz, txh, core, xl),
                )
            )
            q_copies[-1].start()
    for dz in range(8):
        for dxh in range(2):
            for dc in range(2):
                n = dz * 4 + dxh * 2 + dc
                if n == 0:
                    continue
                tc = flip(core, dc)
                l_copies.append(
                    remote(
                        latb.at[tc],
                        lb.at[rows],
                        sem_ls.at[n],
                        sem_lr.at[n],
                        device(y, (z + dz) % 8, flip(xh, dxh), tc, xl),
                    )
                )
                l_copies[-1].start()
    for k in range(8):
        for dxh in range(2):
            for dxl in range(2):
                n = k * 4 + dxh * 2 + dxl
                if n == 0:
                    continue
                ty, tz = ring_b(k)
                o_copies.append(
                    remote(
                        opiece,
                        ob.at[xl * 16 + by_b * 2 + xh],
                        sem_os.at[n],
                        sem_or.at[n],
                        device(ty, tz, flip(xh, dxh), core, flip(xl, dxl)),
                    )
                )
                o_copies[-1].start()

    eb[...] = (lax.broadcasted_iota(jnp.int32, (480, 512), 1) == pick[...]).astype(F32).astype(BF16)
    rows_in[0:64] = wp[...]
    rows_in[64:128] = wft[...]
    for s in range(2):
        c = cond[slot_item[s]]
        hi = c.astype(BF16)
        mid = (c - hi.astype(F32)).astype(BF16)
        low = (c - hi.astype(F32) - mid.astype(F32)).astype(BF16)
        zero = jnp.zeros((3, D), F32)
        for i, piece in enumerate((hi, mid, low)):
            at = 128 + s * 24 + i * 8
            cperm[at - 128 : at - 120] = jnp.concatenate([piece.astype(F32), zero], 0)
    rows_in[128:176] = cperm[0:48].astype(BF16)
    for i in range(6):
        cols = slice(i * 256, (i + 1) * 256)
        onehot = (
            (lax.broadcasted_iota(jnp.int32, (D, 256), 0) == order[:, cols]).astype(F32).astype(BF16)
        )
        rows_out[:, cols] = jnp.dot(rows_in[...], onehot, preferred_element_type=F32)
    blank = jnp.zeros((64, D), BF16)
    wps[0, 0:64] = rows_out[0:64].astype(BF16)
    wps[0, 64:128] = blank
    wps[1, 0:64] = blank
    wps[1, 64:128] = rows_out[0:64].astype(BF16)
    wfs[0, 0:64] = rows_out[64:128].astype(BF16)
    wfs[0, 64:128] = blank
    wfs[1, 0:64] = blank
    wfs[1, 64:128] = rows_out[64:128].astype(BF16)
    for s in range(2):
        at = 128 + s * 24
        cperm[s * 8 : s * 8 + 8] = (
            rows_out[at : at + 8] + rows_out[at + 8 : at + 16] + rows_out[at + 16 : at + 24]
        )

    for copy in q_copies:
        copy.wait_recv()
    packed = jnp.dot(eb[...], qb[...].reshape(512, 128), preferred_element_type=F32).astype(BF16)
    mine = core * 8 + by_c
    for t in range(5):
        qu[mine, :, t * 128 : (t + 1) * 128] = packed[t * 96 : (t + 1) * 96]

    def unit(step):
        return core * 8 + (by_c + step + 8) % 8

    class Spread:
        def __init__(self, buf, s_sem, r_sem, ps_sem, pr_sem):
            self.buf, self.s, self.r, self.ps, self.pr = buf, s_sem, r_sem, ps_sem, pr_sem
            self.sent, self.come = [], {}
            self.partner = []

        def send(self, n, origin, step):
            ty, tz = ring_c((step + 8) % 8)
            slot = unit(origin)
            c = remote(
                self.buf.at[slot],
                self.buf.at[slot],
                self.s.at[n],
                self.r.at[n],
                device(ty, tz, xh, core, xl),
            )
            c.start()
            self.sent.append(c)
            self.come[n] = c

        def share(self, n, origin):
            slot = unit(origin)
            c = remote(
                self.buf.at[slot],
                self.buf.at[slot],
                self.ps.at[n],
                self.pr.at[n],
                device(y, z, xh, 1 - core, xl),
            )
            c.start()
            self.partner.append(c)

        def first(self):
            self.send(0, 0, 2)
            self.send(1, 0, -2)
            self.send(2, 0, 1)
            self.send(3, 0, -1)
            self.share(0, 0)

        def second(self):
            self.come[0].wait_recv()
            self.send(4, -2, 1)
            self.send(6, -2, 2)
            self.come[1].wait_recv()
            self.send(5, 2, -1)
            self.share(1, -2)
            self.share(2, 2)
            self.come[2].wait_recv()
            self.share(3, -1)
            self.come[3].wait_recv()
            self.share(4, 1)

        def third(self):
            self.come[4].wait_recv()
            self.share(5, -3)
            self.come[5].wait_recv()
            self.share(6, 3)
            self.come[6].wait_recv()
            self.share(7, -4)

        def last(self):
            for c in self.partner:
                c.wait_recv()

        def close(self):
            for c in self.sent + self.partner:
                c.wait_send()

    qs = Spread(qu, sem_us, sem_ur, sem_ps, sem_pr)
    qs.first()

    def normalise(value):
        mean = jnp.mean(value, -1, keepdims=True)
        centered = value - mean
        return centered * lax.rsqrt(jnp.mean(centered * centered, -1, keepdims=True) + 1e-06)

    for copy in l_copies:
        copy.wait_recv()

    cmine = cperm[pl.ds(pl.multiple_of(core * 8, 8), 8)]
    shift_a, scale_a = cmine[0:1], 1.0 + cmine[1:2]

    def norm_chunk(i, carry):
        x = lb[pl.ds(i * 4, 4)].reshape(64, 128)
        for parity in range(2):
            e = jnp.dot(x, wps[parity], preferred_element_type=F32)
            for rr in range(4):
                part = e[rr * 16 : rr * 16 + 16] + (rowtab[i * 4 + rr] + coltab[parity])
                at = pl.multiple_of(i * 128 + parity * 64 + rr * 16, 16)
                nb[pl.ds(at, 16)] = (normalise(part) * scale_a + shift_a).astype(BF16)
        return carry

    lax.fori_loop(0, 4, norm_chunk, 0)
    qs.second()
    for copy in o_copies:
        copy.wait_recv()
    for half in range(2):
        got = jnp.dot(
            eb[0:288], ob[half * 16 : half * 16 + 16].reshape(512, 128), preferred_element_type=F32
        ).astype(BF16)
        for t in range(3):
            ou[mine, :, half * 384 + t * 128 : half * 384 + (t + 1) * 128] = got[t * 96 : (t + 1) * 96]
    lax.fori_loop(4, 8, norm_chunk, 0)
    ws = Spread(ou, sem_ws, sem_wr, sem_xs, sem_xr)
    ws.first()
    qs.third()
    qs.last()

    def kv_chunk(i, carry):
        at = pl.ds(pl.multiple_of(i * 256, 256), 256)
        weight = qu[:, :, 0:384].reshape(D, 384)
        kvb[at] = jnp.dot(nb[at], weight, preferred_element_type=F32).astype(BF16)
        return carry

    lax.fori_loop(0, 4, kv_chunk, 0)
    queries = jnp.dot(
        nb[pl.ds(pl.multiple_of(z * 128, 128), 128)],
        qu[:, :, 384:640].reshape(D, 256),
        preferred_element_type=F32,
    ).astype(BF16)
    queries = jnp.concatenate([queries, jnp.zeros((128, 128), BF16)], 1)
    ws.second()

    r_id = lax.broadcasted_iota(jnp.int32, (384, 384), 0)
    c_id = lax.broadcasted_iota(jnp.int32, (384, 384), 1)
    pick_key = ((r_id == c_id + 192 * xh) & (c_id < 192)).astype(F32).astype(BF16)
    pick_val = ((r_id == c_id - 192 + 192 * xh) & (c_id >= 192)).astype(F32).astype(BF16)
    place = ((r_id - 192 + 192 * xh == c_id) & (r_id >= 192)).astype(F32).astype(BF16)
    text_rows = (
        jnp.dot(text[core, 0], pick_key, preferred_element_type=F32)
        + jnp.dot(text[core, 1], pick_val, preferred_element_type=F32)
    ).astype(BF16)

    height, width = heights[core], widths[core]
    key_id = lax.broadcasted_iota(jnp.int32, (1, 1024), 1)
    key_row = (key_id // 128) * 4 + (key_id // 16) % 4
    key_col = (key_id % 16) * 2 + (key_id // 64) % 2
    live = (key_row < height) & (key_col < width)
    lane = lax.broadcasted_iota(jnp.int32, (1, 384), 1)
    nt = (((1,), (1,)), ((), ()))
    kv = kvb[...]
    attended = jnp.zeros((128, 384), F32)
    for h in range(3):
        q_h = jnp.where((lane >= 64 * h) & (lane < 64 * h + 64), queries.astype(F32), 0.0).astype(BF16)
        s_text = lax.dot_general(q_h, text_rows, nt, preferred_element_type=F32) * HD ** (-0.5)
        s_img = lax.dot_general(q_h, kv, nt, preferred_element_type=F32) * HD ** (-0.5)
        s_img = jnp.where(live, s_img, -1e30)
        top = jnp.maximum(jnp.max(s_text, -1, keepdims=True), jnp.max(s_img, -1, keepdims=True))
        w_text = jnp.exp(s_text - top)
        w_img = jnp.exp(s_img - top)
        total = jnp.sum(w_text, -1, keepdims=True) + jnp.sum(w_img, -1, keepdims=True)
        acc = jnp.dot(w_text.astype(BF16), text_rows, preferred_element_type=F32) + jnp.dot(
            w_img.astype(BF16), kv, preferred_element_type=F32
        )
        inside = (lane >= 192 + 64 * h) & (lane < 256 + 64 * h)
        attended = attended + jnp.where(inside, acc / total, 0.0)
    placed = jnp.dot(attended.astype(BF16), place, preferred_element_type=F32).astype(BF16)
    for j in range(4):
        for parity in range(2):
            send_att[j, parity * 16 : parity * 16 + 16] = placed[
                parity * 64 + j * 16 : parity * 64 + j * 16 + 16
            ]
    head_at = xl * 2 + xh
    a_copies = []
    for n in range(1, 8):
        txh, tc, txl = flip(xh, n // 4), flip(core, (n // 2) % 2), flip(xl, n % 2)
        a_copies.append(
            remote(
                send_att.at[txh * 2 + tc],
                recv_att.at[core, head_at],
                sem_as.at[n],
                sem_ar.at[n],
                device(y, z, txh, tc, txl),
            )
        )
        a_copies[-1].start()
    recv_att[core, head_at] = send_att[xh * 2 + core]
    ws.third()
    ws.last()
    for copy in a_copies:
        copy.wait_recv()

    step = jnp.zeros((1, 128), F32) + step_index[0].astype(F32)

    def sigma_level(position):
        fraction = 1.0 - position / STEPS
        return 3.0 * fraction / (1.0 + 2.0 * fraction)

    sigma_now = sigma_level(step)
    sigma_next = sigma_level(step + 1.0)

    halves = [
        jnp.concatenate([recv_att[s, 2 * g] + recv_att[s, 2 * g + 1] for s in range(2)], 0) for g in range(2)
    ]
    projected = lax.dot_general(
        jnp.concatenate(halves, 1), ou[...].reshape(D, 768), nt, preferred_element_type=F32
    )
    for s in range(2):
        gate = cperm[s * 8 + 2 : s * 8 + 3]
        shift_f = cperm[s * 8 + 3 : s * 8 + 4]
        scale_f = 1.0 + cperm[s * 8 + 4 : s * 8 + 5]
        velocity = jnp.zeros((16, 128), F32)
        for parity in range(2):
            e = jnp.dot(latb[s], wps[parity], preferred_element_type=F32) + (rowtab[rows] + coltab[parity])
            at = s * 32 + parity * 16
            residual = e + gate * projected[at : at + 16]
            final_in = (normalise(residual) * scale_f + shift_f).astype(BF16)
            velocity = velocity + lax.dot_general(final_in, wfs[parity], nt, preferred_element_type=F32)
        m_id = lax.broadcasted_iota(jnp.int32, (16, 128), 0)
        l_id = lax.broadcasted_iota(jnp.int32, (16, 128), 1)
        row_live = jnp.where(rows < heights[s], 1, 0)
        alive = (m_id * 2 + l_id // 64 < widths[s] * row_live)
        velocity = jnp.where(alive, velocity, 0.0)
        next_out[s] = lat[s] + (sigma_next - sigma_now) * velocity
        den_out[s] = lat[s] - sigma_now * velocity

    for copy in q_copies + l_copies + o_copies + a_copies:
        copy.wait_send()
    qs.close()
    ws.close()


def body(
    latents,
    heights,
    widths,
    slot_item,
    step_index,
    cond_table,
    text_kv,
    patch_weight,
    qkv_weight,
    out_weight,
    final_weight,
):
    order, pick, rowtab, coltab = tables()
    lat = latents.reshape(2, 16, 128)
    latb = lat.astype(BF16)
    w = jnp.stack([qkv_weight[1], qkv_weight[2], qkv_weight[0]])
    w = w.reshape(3, 6, 2, 192).transpose(2, 1, 0, 3).reshape(2, 6, 576)
    w = jnp.pad(w, ((0, 0), (0, 0), (0, 64))).reshape(2, 6, 5, 128).transpose(0, 2, 1, 3)
    qpiece = jnp.pad(w.reshape(2, 30, 128), ((0, 0), (0, 2), (0, 0)))
    o = out_weight.T.reshape(6, 3, 128).transpose(1, 0, 2).reshape(18, 128)
    opiece = jnp.pad(o, ((0, 14), (0, 0)))
    smem = pl.BlockSpec(memory_space=pltpu.SMEM)
    vmem = pl.BlockSpec(memory_space=pltpu.VMEM)
    dma = pltpu.SemaphoreType.DMA
    shape = jax.ShapeDtypeStruct((2, 16, 128), F32)
    outs = pl.pallas_call(
        kernel,
        out_shape=(shape, shape),
        in_specs=[smem] * 4 + [vmem] * 12,
        out_specs=(vmem, vmem),
        scratch_shapes=[
            pltpu.VMEM((32, 16, 128), BF16),
            pltpu.VMEM((16, 32, 128), BF16),
            pltpu.VMEM((32, 32, 128), BF16),
            pltpu.VMEM((16, UR, 640), BF16),
            pltpu.VMEM((16, UR, 768), BF16),
            pltpu.VMEM((1024, D), BF16),
            pltpu.VMEM((1024, 384), BF16),
            pltpu.VMEM((2, 128, D), BF16),
            pltpu.VMEM((2, 128, D), BF16),
            pltpu.VMEM((48, D), F32),
            pltpu.VMEM((176, D), BF16),
            pltpu.VMEM((176, D), F32),
            pltpu.VMEM((480, 512), BF16),
            pltpu.VMEM((4, 32, 384), BF16),
            pltpu.VMEM((2, 4, 32, 384), BF16),
        ]
        + [dma((n,)) for n in (32, 32, 16, 16, 32, 32, 7, 7, 8, 8, 7, 7, 8, 8, 8, 8)],
        compiler_params=pltpu.CompilerParams(
            collective_id=0, has_side_effects=True, vmem_limit_bytes=56 * 1024 * 1024
        ),
    )(
        heights,
        widths,
        slot_item,
        step_index,
        lat,
        latb,
        cond_table,
        text_kv,
        patch_weight,
        final_weight.T,
        qpiece,
        opiece,
        jnp.asarray(order),
        jnp.asarray(pick),
        jnp.asarray(rowtab),
        jnp.asarray(coltab),
    )
    return tuple(o.reshape(2, 1, 2048) for o in outs)


def solution(mesh):
    return jax.shard_map(
        body,
        mesh=mesh,
        in_specs=(
            P("item", "rows", None),
            P("item"),
            P("item"),
            P("item"),
            P(),
            P(),
            P("item", None, None, "hid"),
            P(),
            P(None, ("item", "rows"), "hid"),
            P("hid", ("item", "rows")),
            P(),
        ),
        out_specs=(P("item", "rows", None), P("item", "rows", None)),
        check_vma=False,
    )
```

```python
import functools

import jax
import jax.numpy as jnp
import numpy as np
from jax import lax
from jax.experimental import pallas as pl
from jax.experimental.pallas import tpu as pltpu
from jax.sharding import PartitionSpec as P

MESH = pl.DeviceIdType.MESH
HD = 64
STEPS = 28
D = 1536
NY, NZ = 8, 8
UR = 96
F32, BF16 = jnp.float32, jnp.bfloat16


def feature_order():
    order = np.zeros((D,), np.int32)
    at = 0
    for core in range(2):
        for outer in range(8):
            for inner in range(8):
                y, z = (outer, inner) if core == 0 else (inner, outer)
                for xh in range(2):
                    block = y * 32 + z * 4 + xh * 2 + core
                    order[at : at + 6] = 6 * block + np.arange(6)
                    at += 6
    return order


def tables():
    order = feature_order()
    quarter = D // 4
    frequency = (
        np.float32(1.0) / np.float32(10000.0) ** (np.arange(quarter, dtype=np.float32) / np.float32(quarter))
    ).astype(np.float32)
    angle = np.arange(32, dtype=np.float32)[:, None] * frequency[None, :]
    part = np.concatenate([np.sin(angle.astype(np.float64)), np.cos(angle.astype(np.float64))], 1)
    zero = np.zeros_like(part)
    row_table = np.concatenate([part, zero], 1)[:, order].astype(np.float32)
    col_table = np.concatenate([zero, part], 1)[:, order].astype(np.float32)
    pick = np.zeros((480, 1), np.int32)
    for tile in range(5):
        for source in range(16):
            for j in range(6):
                pick[tile * 96 + source * 6 + j, 0] = source * 32 + tile * 6 + j
    col_table = np.stack([col_table[0::2], col_table[1::2]])
    return order[None, :], pick, row_table[:, None, :], col_table


def sigma_level(position):
    fraction = 1.0 - position / STEPS
    return 3.0 * fraction / (1.0 + 2.0 * fraction)


def relative_partners():
    found = set()
    for dy in range(NY):
        for dz in range(NZ):
            for dxh in range(2):
                for dc in range(2):
                    for dxl in range(2):
                        near = (dy == 0 and dxl == 0) or (dy == 0 and dz == 0)
                        near = near or (dc == 0 and (dy == 0 or dz == 0))
                        if near:
                            found.add((dy, dz, dxh, dc, dxl))
    found.discard((0, 0, 0, 0, 0))
    return sorted(found)


def kernel(
    heights,
    widths,
    slot_item,
    lat_in,
    cond_in,
    text_in,
    wp_in,
    wft_in,
    wq_in,
    wo_in,
    order_in,
    pick_in,
    rowtab_in,
    coltab_in,
    vel_out,
    lat,
    cond,
    text,
    wp,
    wft,
    wq,
    wo,
    order,
    pick,
    rowtab,
    coltab,
    latb,
    qpiece,
    opiece,
    piece,
    lb,
    qb,
    ob,
    qu,
    ou,
    nb,
    kvb,
    wps,
    wfs,
    cperm,
    rows_in,
    rows_out,
    eb,
    send_att,
    recv_att,
    sem_in,
    sem_ls,
    sem_lr,
    sem_qs,
    sem_qr,
    sem_os,
    sem_or,
    sem_us,
    sem_ur,
    sem_ps,
    sem_pr,
    sem_ws,
    sem_wr,
    sem_xs,
    sem_xr,
    sem_as,
    sem_ar,
):
    y = lax.axis_index("item")
    rows = lax.axis_index("rows")
    xl = lax.axis_index("hid")
    z = rows // 4
    xh = (rows // 2) % 2
    core = rows % 2
    by_b = z * (1 - core) + y * core
    by_c = y * (1 - core) + z * core

    def flip(bit, change):
        return bit if change == 0 else 1 - bit

    def device(ty, tz, txh, tc, txl):
        return (ty, tz * 4 + txh * 2 + tc, txl)

    def ring_b(k):
        return (y + core * k) % 8, (z + (1 - core) * k) % 8

    def ring_c(k):
        return (y + (1 - core) * k) % 8, (z + core * k) % 8

    barrier = pltpu.get_barrier_semaphore()
    partners = relative_partners()
    for dy, dz, dxh, dc, dxl in partners:
        pl.semaphore_signal(
            barrier,
            inc=1,
            device_id=device((y + dy) % 8, (z + dz) % 8, flip(xh, dxh), flip(core, dc), flip(xl, dxl)),
            device_id_type=MESH,
        )
    pairs = (
        (wq_in, wq),
        (wo_in, wo),
        (lat_in, lat),
        (wp_in, wp),
        (wft_in, wft),
        (order_in, order),
        (pick_in, pick),
        (cond_in, cond),
        (rowtab_in, rowtab),
        (coltab_in, coltab),
        (text_in.at[core], text),
    )
    loads = [pltpu.make_async_copy(a, b, sem_in.at[i]) for i, (a, b) in enumerate(pairs)]
    for load in loads:
        load.start()
    loads[0].wait()
    for q in range(2):
        cut = slice(q * 192, (q + 1) * 192)
        parts = [wq[i].astype(F32)[:, cut] for i in (1, 2, 0)]
        full = jnp.concatenate(parts + [jnp.zeros((6, 64), F32)], 1)
        for t in range(5):
            piece[q, t * 6 : t * 6 + 6] = full[:, t * 128 : (t + 1) * 128]
        piece[q, 30:32] = jnp.zeros((2, 128), F32)
        qpiece[q] = piece[q].astype(BF16)
    loads[1].wait()
    for t in range(3):
        piece[2, t * 6 : t * 6 + 6] = wo[:, t * 128 : (t + 1) * 128].astype(F32)
    piece[2, 18:32] = jnp.zeros((14, 128), F32)
    opiece[...] = piece[2].astype(BF16)
    loads[2].wait()
    latb[...] = lat[...].astype(BF16)
    lb[rows] = latb[core]
    qb[by_b * 2 + xh] = qpiece[xh]
    ob[xl * 16 + by_b * 2 + xh] = opiece[...]
    pl.semaphore_wait(barrier, len(partners))

    def remote(src, dst, s_sem, r_sem, to):
        return pltpu.make_async_remote_copy(
            src_ref=src, dst_ref=dst, send_sem=s_sem, recv_sem=r_sem, device_id=to, device_id_type=MESH
        )

    q_copies, l_copies, o_copies = [], [], []
    for k in range(8):
        for dxh in range(2):
            if k == 0 and dxh == 0:
                continue
            ty, tz = ring_b(k)
            txh = flip(xh, dxh)
            n = k * 2 + dxh
            q_copies.append(
                remote(
                    qpiece.at[txh],
                    qb.at[by_b * 2 + xh],
                    sem_qs.at[n],
                    sem_qr.at[n],
                    device(ty, tz, txh, core, xl),
                )
            )
            q_copies[-1].start()
    for dz in range(8):
        for dxh in range(2):
            for dc in range(2):
                n = dz * 4 + dxh * 2 + dc
                if n == 0:
                    continue
                tc = flip(core, dc)
                l_copies.append(
                    remote(
                        latb.at[tc],
                        lb.at[rows],
                        sem_ls.at[n],
                        sem_lr.at[n],
                        device(y, (z + dz) % 8, flip(xh, dxh), tc, xl),
                    )
                )
                l_copies[-1].start()
    for load in loads[3:]:
        load.wait()
    eb[...] = (lax.broadcasted_iota(jnp.int32, (480, 512), 1) == pick[...]).astype(F32).astype(BF16)
    rows_in[0:64] = wp[...]
    rows_in[64:128] = wft[...]
    for s in range(2):
        c = jnp.concatenate([cond[i, pl.ds(slot_item[s], 1)] for i in range(5)], 0)
        hi = c.astype(BF16)
        mid = (c - hi.astype(F32)).astype(BF16)
        low = (c - hi.astype(F32) - mid.astype(F32)).astype(BF16)
        zero = jnp.zeros((3, D), F32)
        for i, piece in enumerate((hi, mid, low)):
            at = 128 + s * 24 + i * 8
            cperm[at - 128 : at - 120] = jnp.concatenate([piece.astype(F32), zero], 0)
    rows_in[128:176] = cperm[0:48].astype(BF16)
    for i in range(6):
        cols = slice(i * 256, (i + 1) * 256)
        onehot = (
            (lax.broadcasted_iota(jnp.int32, (D, 256), 0) == order[:, cols]).astype(F32).astype(BF16)
        )
        rows_out[:, cols] = jnp.dot(rows_in[...], onehot, preferred_element_type=F32)
    blank = jnp.zeros((64, D), BF16)
    wps[0, 0:64] = rows_out[0:64].astype(BF16)
    wps[0, 64:128] = blank
    wps[1, 0:64] = blank
    wps[1, 64:128] = rows_out[0:64].astype(BF16)
    wfs[0, 0:64] = rows_out[64:128].astype(BF16)
    wfs[0, 64:128] = blank
    wfs[1, 0:64] = blank
    wfs[1, 64:128] = rows_out[64:128].astype(BF16)
    for s in range(2):
        at = 128 + s * 24
        cperm[s * 8 : s * 8 + 8] = (
            rows_out[at : at + 8] + rows_out[at + 8 : at + 16] + rows_out[at + 16 : at + 24]
        )

    for copy in q_copies:
        copy.wait_recv()
    packed = jnp.dot(eb[...], qb[...].reshape(512, 128), preferred_element_type=F32).astype(BF16)
    mine = core * 8 + by_c
    for t in range(5):
        qu[mine, :, t * 128 : (t + 1) * 128] = packed[t * 96 : (t + 1) * 96]

    def unit(step):
        return core * 8 + (by_c + step + 8) % 8

    class Spread:
        def __init__(self, buf, s_sem, r_sem, ps_sem, pr_sem):
            self.buf, self.s, self.r, self.ps, self.pr = buf, s_sem, r_sem, ps_sem, pr_sem
            self.sent, self.come = [], {}
            self.partner = []

        def send(self, n, origin, step, part=slice(None)):
            ty, tz = ring_c((step + 8) % 8)
            block = self.buf.at[unit(origin), part]
            c = remote(
                block,
                block,
                self.s.at[n],
                self.r.at[n],
                device(ty, tz, xh, core, xl),
            )
            c.start()
            self.sent.append(c)
            self.come[n] = c

        def share(self, n, origin):
            slot = unit(origin)
            c = remote(
                self.buf.at[slot],
                self.buf.at[slot],
                self.ps.at[n],
                self.pr.at[n],
                device(y, z, xh, 1 - core, xl),
            )
            c.start()
            self.partner.append(c)

        def first(self):
            self.send(0, 0, 2)
            self.send(1, 0, -2)
            self.send(2, 0, 1)
            self.send(3, 0, -1)
            self.share(0, 0)

        def second(self):
            self.come[0].wait_recv()
            self.send(4, -2, 1)
            self.send(6, -2, 2, slice(0, 48))
            self.come[1].wait_recv()
            self.send(5, 2, -1)
            self.send(7, 2, -2, slice(48, 96))
            self.share(1, -2)
            self.share(2, 2)
            self.come[2].wait_recv()
            self.share(3, -1)
            self.come[3].wait_recv()
            self.share(4, 1)

        def third(self):
            self.come[4].wait_recv()
            self.share(5, -3)
            self.come[5].wait_recv()
            self.share(6, 3)
            self.come[6].wait_recv()
            self.come[7].wait_recv()
            self.share(7, -4)

        def last(self):
            for c in self.partner:
                c.wait_recv()

        def close(self):
            for c in self.sent + self.partner:
                c.wait_send()

    qs = Spread(qu, sem_us, sem_ur, sem_ps, sem_pr)
    qs.first()
    for k in range(8):
        for dxh in range(2):
            for dxl in range(2):
                n = k * 4 + dxh * 2 + dxl
                if n == 0:
                    continue
                ty, tz = ring_b(k)
                o_copies.append(
                    remote(
                        opiece,
                        ob.at[xl * 16 + by_b * 2 + xh],
                        sem_os.at[n],
                        sem_or.at[n],
                        device(ty, tz, flip(xh, dxh), core, flip(xl, dxl)),
                    )
                )
                o_copies[-1].start()


    r_id = lax.broadcasted_iota(jnp.int32, (384, 384), 0)
    c_id = lax.broadcasted_iota(jnp.int32, (384, 384), 1)
    pick_key = ((r_id == c_id + 192 * xh) & (c_id < 192)).astype(F32).astype(BF16)
    pick_val = ((r_id == c_id - 192 + 192 * xh) & (c_id >= 192)).astype(F32).astype(BF16)
    place = ((r_id - 192 + 192 * xh == c_id) & (r_id >= 192)).astype(F32).astype(BF16)
    text_rows = (
        jnp.dot(text[:, 0], pick_key, preferred_element_type=F32)
        + jnp.dot(text[:, 1], pick_val, preferred_element_type=F32)
    ).astype(BF16)

    def normalise(value):
        mean = jnp.mean(value, -1, keepdims=True)
        centered = value - mean
        return centered * lax.rsqrt(jnp.mean(centered * centered, -1, keepdims=True) + 1e-06)

    for copy in l_copies:
        copy.wait_recv()

    cmine = cperm[pl.ds(pl.multiple_of(core * 8, 8), 8)]
    shift_a, scale_a = cmine[0:1], 1.0 + cmine[1:2]

    def norm_chunk(i, carry):
        x = lb[pl.ds(i * 4, 4)].reshape(64, 128)
        for parity in range(2):
            e = jnp.dot(x, wps[parity], preferred_element_type=F32)
            for rr in range(4):
                part = e[rr * 16 : rr * 16 + 16] + (rowtab[i * 4 + rr] + coltab[parity])
                at = pl.multiple_of(i * 128 + parity * 64 + rr * 16, 16)
                nb[pl.ds(at, 16)] = (normalise(part) * scale_a + shift_a).astype(BF16)
        return carry

    lax.fori_loop(0, 4, norm_chunk, 0)
    qs.second()
    for copy in o_copies:
        copy.wait_recv()
    for half in range(2):
        got = jnp.dot(
            eb[0:288], ob[half * 16 : half * 16 + 16].reshape(512, 128), preferred_element_type=F32
        ).astype(BF16)
        for t in range(3):
            ou[mine, :, half * 384 + t * 128 : half * 384 + (t + 1) * 128] = got[t * 96 : (t + 1) * 96]
    lax.fori_loop(4, 8, norm_chunk, 0)
    ws = Spread(ou, sem_ws, sem_wr, sem_xs, sem_xr)
    ws.first()
    qs.third()
    qs.last()

    def kv_chunk(i, carry):
        at = pl.ds(pl.multiple_of(i * 256, 256), 256)
        weight = qu[:, :, 0:384].reshape(D, 384)
        kvb[at] = jnp.dot(nb[at], weight, preferred_element_type=F32).astype(BF16)
        return carry

    lax.fori_loop(0, 4, kv_chunk, 0)
    queries = jnp.dot(
        nb[pl.ds(pl.multiple_of(z * 128, 128), 128)],
        qu[:, :, 384:640].reshape(D, 256),
        preferred_element_type=F32,
    ).astype(BF16)
    queries = jnp.concatenate([queries, jnp.zeros((128, 128), BF16)], 1)
    ws.second()

    height, width = heights[core], widths[core]
    key_id = lax.broadcasted_iota(jnp.int32, (1, 1024), 1)
    key_row = (key_id // 128) * 4 + (key_id // 16) % 4
    key_col = (key_id % 16) * 2 + (key_id // 64) % 2
    live = (key_row < height) & (key_col < width)
    lane = lax.broadcasted_iota(jnp.int32, (1, 384), 1)
    nt = (((1,), (1,)), ((), ()))
    kv = kvb[...]
    attended = jnp.zeros((128, 384), F32)
    for h in range(3):
        q_h = jnp.where((lane >= 64 * h) & (lane < 64 * h + 64), queries.astype(F32), 0.0).astype(BF16)
        s_text = lax.dot_general(q_h, text_rows, nt, preferred_element_type=F32) * HD ** (-0.5)
        s_img = lax.dot_general(q_h, kv, nt, preferred_element_type=F32) * HD ** (-0.5)
        s_img = jnp.where(live, s_img, -1e30)
        top = jnp.maximum(jnp.max(s_text, -1, keepdims=True), jnp.max(s_img, -1, keepdims=True))
        w_text = jnp.exp(s_text - top)
        w_img = jnp.exp(s_img - top)
        total = jnp.sum(w_text, -1, keepdims=True) + jnp.sum(w_img, -1, keepdims=True)
        acc = jnp.dot(w_text.astype(BF16), text_rows, preferred_element_type=F32) + jnp.dot(
            w_img.astype(BF16), kv, preferred_element_type=F32
        )
        inside = (lane >= 192 + 64 * h) & (lane < 256 + 64 * h)
        attended = attended + jnp.where(inside, acc / total, 0.0)
    placed = jnp.dot(attended.astype(BF16), place, preferred_element_type=F32).astype(BF16)
    for j in range(4):
        for parity in range(2):
            send_att[j, parity * 16 : parity * 16 + 16] = placed[
                parity * 64 + j * 16 : parity * 64 + j * 16 + 16
            ]
    head_at = xl * 2 + xh
    a_copies = []
    for n in range(1, 8):
        txh, tc, txl = flip(xh, n // 4), flip(core, (n // 2) % 2), flip(xl, n % 2)
        a_copies.append(
            remote(
                send_att.at[txh * 2 + tc],
                recv_att.at[core, head_at],
                sem_as.at[n],
                sem_ar.at[n],
                device(y, z, txh, tc, txl),
            )
        )
        a_copies[-1].start()
    recv_att[core, head_at] = send_att[xh * 2 + core]
    ws.third()
    ws.last()
    for copy in a_copies:
        copy.wait_recv()

    halves = [
        jnp.concatenate([recv_att[s, 2 * g] + recv_att[s, 2 * g + 1] for s in range(2)], 0) for g in range(2)
    ]
    projected = lax.dot_general(
        jnp.concatenate(halves, 1), ou[...].reshape(D, 768), nt, preferred_element_type=F32
    )
    for s in range(2):
        gate = cperm[s * 8 + 2 : s * 8 + 3]
        shift_f = cperm[s * 8 + 3 : s * 8 + 4]
        scale_f = 1.0 + cperm[s * 8 + 4 : s * 8 + 5]
        velocity = jnp.zeros((16, 128), F32)
        for parity in range(2):
            e = jnp.dot(latb[s], wps[parity], preferred_element_type=F32) + (rowtab[rows] + coltab[parity])
            at = s * 32 + parity * 16
            residual = e + gate * projected[at : at + 16]
            final_in = (normalise(residual) * scale_f + shift_f).astype(BF16)
            velocity = velocity + lax.dot_general(final_in, wfs[parity], nt, preferred_element_type=F32)
        m_id = lax.broadcasted_iota(jnp.int32, (16, 128), 0)
        l_id = lax.broadcasted_iota(jnp.int32, (16, 128), 1)
        row_live = jnp.where(rows < heights[s], 1, 0)
        alive = (m_id * 2 + l_id // 64 < widths[s] * row_live)
        vel_out[s] = jnp.where(alive, velocity, 0.0)

    for copy in q_copies + l_copies + o_copies + a_copies:
        copy.wait_send()
    qs.close()
    ws.close()


def body(
    latents,
    heights,
    widths,
    slot_item,
    step_index,
    cond_table,
    text_kv,
    patch_weight,
    qkv_weight,
    out_weight,
    final_weight,
):
    order, pick, rowtab, coltab = tables()
    smem = pl.BlockSpec(memory_space=pltpu.SMEM)
    vmem = pl.BlockSpec(memory_space=pltpu.VMEM)
    dma = pltpu.SemaphoreType.DMA
    shape = jax.ShapeDtypeStruct((2, 16, 128), F32)
    velocity = pl.pallas_call(
        kernel,
        out_shape=shape,
        in_specs=[smem] * 3 + [pl.BlockSpec(memory_space=pl.ANY)] * 11,
        out_specs=vmem,
        scratch_shapes=[
            pltpu.VMEM((2, 16, 128), F32),
            pltpu.VMEM((5, 16, D), F32),
            pltpu.VMEM((154, 2, 384), BF16),
            pltpu.VMEM((64, D), BF16),
            pltpu.VMEM((64, D), BF16),
            pltpu.VMEM((3, 6, 384), BF16),
            pltpu.VMEM((6, 384), BF16),
            pltpu.VMEM(order.shape, jnp.int32),
            pltpu.VMEM(pick.shape, jnp.int32),
            pltpu.VMEM(rowtab.shape, F32),
            pltpu.VMEM(coltab.shape, F32),
            pltpu.VMEM((2, 16, 128), BF16),
            pltpu.VMEM((2, 32, 128), BF16),
            pltpu.VMEM((32, 128), BF16),
            pltpu.VMEM((3, 32, 128), F32),
            pltpu.VMEM((32, 16, 128), BF16),
            pltpu.VMEM((16, 32, 128), BF16),
            pltpu.VMEM((32, 32, 128), BF16),
            pltpu.VMEM((16, UR, 640), BF16),
            pltpu.VMEM((16, UR, 768), BF16),
            pltpu.VMEM((1024, D), BF16),
            pltpu.VMEM((1024, 384), BF16),
            pltpu.VMEM((2, 128, D), BF16),
            pltpu.VMEM((2, 128, D), BF16),
            pltpu.VMEM((48, D), F32),
            pltpu.VMEM((176, D), BF16),
            pltpu.VMEM((176, D), F32),
            pltpu.VMEM((480, 512), BF16),
            pltpu.VMEM((4, 32, 384), BF16),
            pltpu.VMEM((2, 4, 32, 384), BF16),
        ]
        + [dma((n,)) for n in (11, 32, 32, 16, 16, 32, 32, 8, 8, 8, 8, 8, 8, 8, 8, 8, 8)],
        compiler_params=pltpu.CompilerParams(
            collective_id=0, has_side_effects=True, vmem_limit_bytes=56 * 1024 * 1024
        ),
    )(
        heights,
        widths,
        slot_item,
        latents.reshape(2, 16, 128),
        cond_table.transpose(1, 0, 2),
        text_kv.transpose(0, 2, 1, 3),
        patch_weight,
        final_weight.T,
        qkv_weight,
        out_weight.T,
        jnp.asarray(order),
        jnp.asarray(pick),
        jnp.asarray(rowtab),
        jnp.asarray(coltab),
    ).reshape(2, 1, 2048)
    position = step_index[0].astype(F32)
    sigma_now = sigma_level(position)
    sigma_next = sigma_level(position + 1.0)
    return latents + (sigma_next - sigma_now) * velocity, latents - sigma_now * velocity


def solution(mesh):
    return jax.shard_map(
        body,
        mesh=mesh,
        in_specs=(
            P("item", "rows", None),
            P("item"),
            P("item"),
            P("item"),
            P(),
            P(),
            P("item", None, None, "hid"),
            P(),
            P(None, ("item", "rows"), "hid"),
            P("hid", ("item", "rows")),
            P(),
        ),
        out_specs=(P("item", "rows", None), P("item", "rows", None)),
        check_vma=False,
    )
```

```python
import functools

import jax
import jax.numpy as jnp
import numpy as np
from jax import lax
from jax.experimental import pallas as pl
from jax.experimental.pallas import tpu as pltpu
from jax.sharding import PartitionSpec as P

MESH = pl.DeviceIdType.MESH
HD = 64
STEPS = 28
D = 1536
NY, NZ = 8, 8
UR = 96
F32, BF16 = jnp.float32, jnp.bfloat16


def feature_order():
    order = np.zeros((D,), np.int32)
    at = 0
    for core in range(2):
        for outer in range(8):
            for inner in range(8):
                y, z = (outer, inner) if core == 0 else (inner, outer)
                for xh in range(2):
                    block = y * 32 + z * 4 + xh * 2 + core
                    order[at : at + 6] = 6 * block + np.arange(6)
                    at += 6
    return order


def tables():
    order = feature_order()
    quarter = D // 4
    frequency = (
        np.float32(1.0) / np.float32(10000.0) ** (np.arange(quarter, dtype=np.float32) / np.float32(quarter))
    ).astype(np.float32)
    angle = np.arange(32, dtype=np.float32)[:, None] * frequency[None, :]
    part = np.concatenate([np.sin(angle.astype(np.float64)), np.cos(angle.astype(np.float64))], 1)
    zero = np.zeros_like(part)
    row_table = np.concatenate([part, zero], 1)[:, order].astype(np.float32)
    col_table = np.concatenate([zero, part], 1)[:, order].astype(np.float32)
    pick = np.zeros((480, 1), np.int32)
    for tile in range(5):
        for source in range(16):
            for j in range(6):
                pick[tile * 96 + source * 6 + j, 0] = source * 32 + tile * 6 + j
    pick_out = np.zeros((144, 1), np.int32)
    for tile in range(3):
        for source in range(16):
            for j in range(3):
                pick_out[tile * 48 + source * 3 + j, 0] = source * 16 + tile * 3 + j
    col_table = np.stack([col_table[0::2], col_table[1::2]])
    place = np.arange(D).reshape(256, 2, 3)
    halves = np.stack([place[:, h].reshape(-1) for h in range(2)])
    return (
        order[None, :],
        pick,
        row_table[:, None, :],
        col_table,
        order[halves][:, None, :],
        pick_out,
        np.stack([row_table[:, None, half] for half in halves]),
        np.stack([col_table[:, :, half] for half in halves]),
    )


def sigma_level(position):
    fraction = 1.0 - position / STEPS
    return 3.0 * fraction / (1.0 + 2.0 * fraction)


def relative_partners():
    found = set()
    for dy in range(NY):
        for dz in range(NZ):
            for dxh in range(2):
                for dc in range(2):
                    for dxl in range(2):
                        near = (dy == 0 and dxl == 0 and dxh == 0) or (dy == 0 and dz == 0)
                        near = near or (dc == 0 and (dy == 0 or dz == 0))
                        if near:
                            found.add((dy, dz, dxh, dc, dxl))
    found.discard((0, 0, 0, 0, 0))
    return sorted(found)


def kernel(
    heights_in,
    widths_in,
    slot_in,
    lat_in,
    cond_in,
    text_in,
    wp_in,
    wft_in,
    wq_in,
    wo_in,
    order_in,
    pick_in,
    rowtab_in,
    coltab_in,
    order_h_in,
    pick_o_in,
    rowtab_h_in,
    coltab_h_in,
    vel_out,
    heights,
    widths,
    slot_item,
    lat,
    cond,
    text,
    wp,
    wft,
    wq,
    wo,
    order,
    pick,
    rowtab,
    coltab,
    order_h,
    pick_o,
    rowtab_h,
    coltab_h,
    latb,
    qpiece,
    opiece,
    piece,
    lb,
    qb,
    ob,
    qu,
    ou,
    nb,
    kvb,
    wps,
    wph,
    wfh,
    cperm,
    chalf,
    split,
    sums_in,
    rows_in,
    rows_out,
    rows_half,
    eb,
    eo,
    send_att,
    recv_att,
    pay,
    got_pay,
    sem_in,
    sem_ls,
    sem_lr,
    sem_qs,
    sem_qr,
    sem_os,
    sem_or,
    sem_us,
    sem_ur,
    sem_ps,
    sem_pr,
    sem_ws,
    sem_wr,
    sem_xs,
    sem_xr,
    sem_as,
    sem_ar,
    sem_bs,
    sem_br,
    sem_fs,
    sem_fr,
):
    y = lax.axis_index("item")
    rows = lax.axis_index("rows")
    xl = lax.axis_index("hid")
    z = rows // 4
    xh = (rows // 2) % 2
    core = rows % 2
    by_b = z * (1 - core) + y * core
    by_c = y * (1 - core) + z * core

    def flip(bit, change):
        return bit if change == 0 else 1 - bit

    def device(ty, tz, txh, tc, txl):
        return (ty, tz * 4 + txh * 2 + tc, txl)

    def ring_b(k):
        return (y + core * k) % 8, (z + (1 - core) * k) % 8

    def ring_c(k):
        return (y + (1 - core) * k) % 8, (z + core * k) % 8

    barrier = pltpu.get_barrier_semaphore()
    partners = relative_partners()
    for dy, dz, dxh, dc, dxl in partners:
        pl.semaphore_signal(
            barrier,
            inc=1,
            device_id=device((y + dy) % 8, (z + dz) % 8, flip(xh, dxh), flip(core, dc), flip(xl, dxl)),
            device_id_type=MESH,
        )
    pairs = (
        (wq_in, wq),
        (wo_in, wo),
        (lat_in, lat),
        (wp_in, wp),
        (wft_in, wft),
        (order_in, order),
        (pick_in, pick),
        (cond_in, cond),
        (rowtab_in, rowtab),
        (coltab_in, coltab),
        (text_in.at[core], text),
        (order_h_in.at[xl], order_h),
        (pick_o_in, pick_o),
        (rowtab_h_in.at[xl], rowtab_h),
        (coltab_h_in.at[xl], coltab_h),
        (heights_in, heights),
        (widths_in, widths),
        (slot_in, slot_item),
    )
    loads = [pltpu.make_async_copy(a, b, sem_in.at[i]) for i, (a, b) in enumerate(pairs)]
    for load in loads:
        load.start()
    loads[0].wait()
    for q in range(2):
        cut = slice(q * 192, (q + 1) * 192)
        parts = [wq[i].astype(F32)[:, cut] for i in (1, 2, 0)]
        full = jnp.concatenate(parts + [jnp.zeros((6, 64), F32)], 1)
        for t in range(5):
            piece[q, t * 6 : t * 6 + 6] = full[:, t * 128 : (t + 1) * 128]
        piece[q, 30:32] = jnp.zeros((2, 128), F32)
        qpiece[q] = piece[q].astype(BF16)
    loads[1].wait()
    for half in range(2):
        for t in range(3):
            at = half * 16 + t * 3
            piece[2, at : at + 3] = wo[...].astype(F32)[half * 3 : half * 3 + 3, t * 128 : (t + 1) * 128]
        piece[2, half * 16 + 9 : half * 16 + 16] = jnp.zeros((7, 128), F32)
        opiece[half] = piece[2, half * 16 : half * 16 + 16].astype(BF16)
    loads[2].wait()
    latb[...] = lat[...].astype(BF16)
    my_lat = xh * 16 + z * 2 + core
    lb[my_lat] = latb[core]
    qb[by_b * 2 + xh] = qpiece[xh]
    ob[xl * 16 + by_b * 2 + xh] = opiece[xl]
    pl.semaphore_wait(barrier, len(partners))

    def remote(src, dst, s_sem, r_sem, to):
        return pltpu.make_async_remote_copy(
            src_ref=src, dst_ref=dst, send_sem=s_sem, recv_sem=r_sem, device_id=to, device_id_type=MESH
        )

    q_copies, l_copies, o_copies = [], [], []
    for k in range(8):
        for dxh in range(2):
            if k == 0 and dxh == 0:
                continue
            ty, tz = ring_b(k)
            txh = flip(xh, dxh)
            n = k * 2 + dxh
            q_copies.append(
                remote(
                    qpiece.at[txh],
                    qb.at[by_b * 2 + xh],
                    sem_qs.at[n],
                    sem_qr.at[n],
                    device(ty, tz, txh, core, xl),
                )
            )
            q_copies[-1].start()
    for dz in range(8):
        for dc in range(2):
            n = dz * 2 + dc
            if n == 0:
                continue
            tc = flip(core, dc)
            l_copies.append(
                remote(
                    latb.at[tc],
                    lb.at[my_lat],
                    sem_ls.at[n],
                    sem_lr.at[n],
                    device(y, (z + dz) % 8, xh, tc, xl),
                )
            )
            l_copies[-1].start()
    for load in loads[3:]:
        load.wait()
    eb[...] = (lax.broadcasted_iota(jnp.int32, (480, 512), 1) == pick[...]).astype(F32).astype(BF16)
    eo[...] = (lax.broadcasted_iota(jnp.int32, (144, 256), 1) == pick_o[...]).astype(F32).astype(BF16)

    for copy in q_copies:
        copy.wait_recv()
    packed = jnp.dot(eb[...], qb[...].reshape(512, 128), preferred_element_type=F32).astype(BF16)
    mine = core * 8 + by_c
    for t in range(5):
        qu[mine, :, t * 128 : (t + 1) * 128] = packed[t * 96 : (t + 1) * 96]

    def unit(step):
        return core * 8 + (by_c + step + 8) % 8

    class Spread:
        def __init__(self, buf, s_sem, r_sem, ps_sem, pr_sem):
            self.buf, self.s, self.r, self.ps, self.pr = buf, s_sem, r_sem, ps_sem, pr_sem
            self.cut = buf.shape[1] // 32 * 16 + buf.shape[1] % 32
            self.sent, self.come = [], {}
            self.partner = []

        def send(self, n, origin, step, part=slice(None)):
            ty, tz = ring_c((step + 8) % 8)
            block = self.buf.at[unit(origin), part]
            c = remote(
                block,
                block,
                self.s.at[n],
                self.r.at[n],
                device(ty, tz, xh, core, xl),
            )
            c.start()
            self.sent.append(c)
            self.come[n] = c

        def share(self, n, origin):
            slot = unit(origin)
            c = remote(
                self.buf.at[slot],
                self.buf.at[slot],
                self.ps.at[n],
                self.pr.at[n],
                device(y, z, xh, 1 - core, xl),
            )
            c.start()
            self.partner.append(c)

        def first(self):
            self.send(0, 0, 2)
            self.send(1, 0, -2)
            self.send(2, 0, 1)
            self.send(3, 0, -1)
            self.share(0, 0)

        def second(self):
            self.come[0].wait_recv()
            self.send(4, -2, 1)
            self.send(6, -2, 2, slice(0, self.cut))
            self.come[1].wait_recv()
            self.send(5, 2, -1)
            self.send(7, 2, -2, slice(self.cut, None))
            self.share(1, -2)
            self.share(2, 2)
            self.come[2].wait_recv()
            self.share(3, -1)
            self.come[3].wait_recv()
            self.share(4, 1)

        def third(self):
            self.come[4].wait_recv()
            self.share(5, -3)
            self.come[5].wait_recv()
            self.share(6, 3)
            self.come[6].wait_recv()
            self.come[7].wait_recv()
            self.share(7, -4)

        def last(self):
            for c in self.partner:
                c.wait_recv()

        def close(self):
            for c in self.sent + self.partner:
                c.wait_send()

    qs = Spread(qu, sem_us, sem_ur, sem_ps, sem_pr)
    qs.first()
    for k in range(8):
        for dxh in range(2):
            for dxl in range(2):
                n = k * 4 + dxh * 2 + dxl
                if n == 0:
                    continue
                ty, tz = ring_b(k)
                o_copies.append(
                    remote(
                        opiece.at[flip(xl, dxl)],
                        ob.at[xl * 16 + by_b * 2 + xh],
                        sem_os.at[n],
                        sem_or.at[n],
                        device(ty, tz, flip(xh, dxh), core, flip(xl, dxl)),
                    )
                )
                o_copies[-1].start()


    for copy in l_copies:
        copy.wait_recv()
    block = lb.at[pl.ds(pl.multiple_of(xh * 16, 16), 16)]
    b_copy = remote(block, block, sem_bs.at[0], sem_br.at[0], device(y, z, 1 - xh, core, xl))
    b_copy.start()

    rows_in[0:64] = wp[...]
    rows_in[112:176] = wft[...]

    def three(value):
        hi = value.astype(BF16).astype(F32)
        mid = (value - hi).astype(BF16).astype(F32)
        return hi, mid, (value - hi - mid).astype(BF16).astype(F32)

    in_first = (lax.broadcasted_iota(jnp.int32, (1, D), 1) % 6) < 3
    for s in range(2):
        c = jnp.concatenate([cond[i, pl.ds(slot_item[s], 1)] for i in range(5)], 0)
        for i, part in enumerate(three(c)):
            at = s * 24 + i * 8
            split[at : at + 8] = jnp.concatenate([part, jnp.zeros((3, D), F32)], 0)
        scale_f = 1.0 + c[4:5]
        first = jnp.where(in_first, scale_f, 0.0)
        three_rows = jnp.concatenate([first, scale_f - first, c[3:4]], 0)
        parts = three(three_rows)
        sums_in[s * 16 : s * 16 + 16] = jnp.concatenate(list(parts) + [jnp.zeros((7, D), F32)], 0)
    rows_in[64:112] = split[...].astype(BF16)

    def onehot(names):
        return (lax.broadcasted_iota(jnp.int32, (D, 256), 0) == names).astype(F32).astype(BF16)

    for i in range(6):
        cols = slice(i * 256, (i + 1) * 256)
        rows_out[:, cols] = jnp.dot(rows_in[0:112], onehot(order[:, cols]), preferred_element_type=F32)
    for i in range(3):
        cols = slice(i * 256, (i + 1) * 256)
        rows_half[:, cols] = jnp.dot(rows_in[...], onehot(order_h[:, cols]), preferred_element_type=F32)
    for at, rest in ((0, 64), (1, 0)):
        wps[at, at * 64 : at * 64 + 64] = rows_out[0:64].astype(BF16)
        wps[at, rest : rest + 64] = jnp.zeros((64, D), BF16)
        wph[at, at * 64 : at * 64 + 64] = rows_half[0:64].astype(BF16)
        wph[at, rest : rest + 64] = jnp.zeros((64, D // 2), BF16)
        wfh[at, at * 64 : at * 64 + 64] = rows_half[112:176].astype(BF16)
        wfh[at, rest : rest + 64] = jnp.zeros((64, D // 2), BF16)
    for s in range(2):
        at = 64 + s * 24
        for src, dst in ((rows_out, cperm), (rows_half, chalf)):
            dst[s * 8 : s * 8 + 8] = src[at : at + 8] + src[at + 8 : at + 16] + src[at + 16 : at + 24]
    nt = (((1,), (1,)), ((), ()))
    final_rows = jnp.concatenate([wft[...], wft[...]], 0)
    sums = lax.dot_general(sums_in[...].astype(BF16), final_rows, nt, preferred_element_type=F32)

    r_id = lax.broadcasted_iota(jnp.int32, (384, 384), 0)
    c_id = lax.broadcasted_iota(jnp.int32, (384, 384), 1)
    pick_key = ((r_id == c_id + 192 * xh) & (c_id < 192)).astype(F32).astype(BF16)
    pick_val = ((r_id == c_id - 192 + 192 * xh) & (c_id >= 192)).astype(F32).astype(BF16)
    place = ((r_id - 64 + 192 * xh == c_id) & (r_id >= 64)).astype(F32).astype(BF16)[0:256]
    text_rows = (
        jnp.dot(text[:, 0], pick_key, preferred_element_type=F32)
        + jnp.dot(text[:, 1], pick_val, preferred_element_type=F32)
    ).astype(BF16)

    def normalise(value):
        mean = jnp.mean(value, -1, keepdims=True)
        centered = value - mean
        return centered * lax.rsqrt(jnp.mean(centered * centered, -1, keepdims=True) + 1e-06)

    cmine = cperm[pl.ds(pl.multiple_of(core * 8, 8), 8)]
    shift_a, scale_a = cmine[0:1], 1.0 + cmine[1:2]

    def norm_half(half):
        def chunk(i, carry):
            x = lb[pl.ds(half * 16 + i * 4, 4)].reshape(64, 128)
            for parity in range(2):
                e = jnp.dot(x, wps[parity], preferred_element_type=F32)
                for rr in range(4):
                    row = (i * 2 + rr // 2) * 4 + half * 2 + rr % 2
                    part = e[rr * 16 : rr * 16 + 16] + (rowtab[row] + coltab[parity])
                    at = (row // 4) * 128 + parity * 64 + (row % 4) * 16
                    nb[pl.ds(pl.multiple_of(at, 16), 16)] = (normalise(part) * scale_a + shift_a).astype(BF16)
            return carry

        lax.fori_loop(0, 4, chunk, 0)

    norm_half(xh)
    qs.second()
    for copy in o_copies:
        copy.wait_recv()
    for half in range(2):
        got = jnp.dot(
            eo[...], ob[half * 16 : half * 16 + 16].reshape(256, 128), preferred_element_type=F32
        ).astype(BF16)
        for t in range(3):
            ou[mine, :, half * 384 + t * 128 : half * 384 + (t + 1) * 128] = got[t * 48 : (t + 1) * 48]
    ws = Spread(ou, sem_ws, sem_wr, sem_xs, sem_xr)
    ws.first()
    b_copy.wait_recv()
    norm_half(1 - xh)
    qs.third()
    qs.last()

    def kv_chunk(i, carry):
        at = pl.ds(pl.multiple_of(i * 256, 256), 256)
        weight = qu[:, :, 0:384].reshape(D, 384)
        kvb[at] = jnp.dot(nb[at], weight, preferred_element_type=F32).astype(BF16)
        return carry

    lax.fori_loop(0, 4, kv_chunk, 0)
    queries = jnp.dot(
        nb[pl.ds(pl.multiple_of(z * 128, 128), 128)],
        qu[:, :, 384:640].reshape(D, 256),
        preferred_element_type=F32,
    ).astype(BF16)
    ws.second()

    height, width = heights[core], widths[core]
    key_id = lax.broadcasted_iota(jnp.int32, (1, 1024), 1)
    key_row = (key_id // 128) * 4 + (key_id // 16) % 4
    key_col = (key_id % 16) * 2 + (key_id // 64) % 2
    live = (key_row < height) & (key_col < width)
    lane = lax.broadcasted_iota(jnp.int32, (1, 256), 1)
    keys, values = kvb[:, 0:256], kvb[:, 128:384]
    attended = jnp.zeros((128, 256), F32)
    masked = [
        jnp.where((lane >= 64 * h) & (lane < 64 * h + 64), queries.astype(F32), 0.0).astype(BF16) for h in range(3)
    ]
    stacked = jnp.concatenate(masked, 0)
    s_text = lax.dot_general(stacked, text_rows[:, 0:256], nt, preferred_element_type=F32) * HD ** (-0.5)
    s_img = lax.dot_general(stacked, keys, nt, preferred_element_type=F32) * HD ** (-0.5)
    s_img = jnp.where(live, s_img, -1e30)
    top = jnp.maximum(jnp.max(s_text, -1, keepdims=True), jnp.max(s_img, -1, keepdims=True))
    w_text = jnp.exp(s_text - top)
    w_img = jnp.exp(s_img - top)
    total = jnp.sum(w_text, -1, keepdims=True) + jnp.sum(w_img, -1, keepdims=True)
    acc = jnp.dot(w_text.astype(BF16), text_rows[:, 128:384], preferred_element_type=F32) + jnp.dot(
        w_img.astype(BF16), values, preferred_element_type=F32
    )
    acc = acc / total
    for h in range(3):
        inside = (lane >= 64 + 64 * h) & (lane < 128 + 64 * h)
        attended = attended + jnp.where(inside, acc[h * 128 : (h + 1) * 128], 0.0)
    placed = jnp.dot(attended.astype(BF16), place, preferred_element_type=F32).astype(BF16)
    for j in range(4):
        for parity in range(2):
            send_att[j, parity * 16 : parity * 16 + 16] = placed[
                parity * 64 + j * 16 : parity * 64 + j * 16 + 16
            ]
    head_at = xl * 2 + xh
    a_copies = []
    for n in range(1, 8):
        txh, tc, txl = flip(xh, n // 4), flip(core, (n // 2) % 2), flip(xl, n % 2)
        a_copies.append(
            remote(
                send_att.at[txh * 2 + tc],
                recv_att.at[core, head_at],
                sem_as.at[n],
                sem_ar.at[n],
                device(y, z, txh, tc, txl),
            )
        )
        a_copies[-1].start()
    recv_att[core, head_at] = send_att[xh * 2 + core]
    ws.third()
    ws.last()
    for copy in a_copies:
        copy.wait_recv()

    halves = [
        jnp.concatenate([recv_att[s, 2 * g] + recv_att[s, 2 * g + 1] for s in range(2)], 0) for g in range(2)
    ]
    projected = lax.dot_general(
        jnp.concatenate(halves, 1), ou[...].reshape(D // 2, 768), nt, preferred_element_type=F32
    )
    l_id = lax.broadcasted_iota(jnp.int32, (16, 128), 1)
    stats = jnp.zeros((16, 128), F32)
    for s in range(2):
        gate = chalf[s * 8 + 2 : s * 8 + 3]
        scale_f = 1.0 + chalf[s * 8 + 4 : s * 8 + 5]
        product = jnp.zeros((16, 128), F32)
        for parity in range(2):
            e = jnp.dot(latb[s], wph[parity], preferred_element_type=F32) + (rowtab_h[rows] + coltab_h[parity])
            at = s * 32 + parity * 16
            residual = e + gate * projected[at : at + 16]
            mean = jnp.mean(residual, -1, keepdims=True)
            centered = residual - mean
            squares = jnp.sum(centered * centered, -1, keepdims=True)
            stats = jnp.where(l_id == s * 4 + parity * 2, mean, stats)
            stats = jnp.where(l_id == s * 4 + parity * 2 + 1, squares, stats)
            product = product + lax.dot_general(
                (centered * scale_f).astype(BF16), wfh[parity], nt, preferred_element_type=F32
            )
        pay[s] = product
    pay[2] = stats
    f_copy = remote(pay, got_pay, sem_fs.at[0], sem_fr.at[0], device(y, z, xh, core, 1 - xl))
    f_copy.start()
    f_copy.wait_recv()
    stats_0 = jnp.where(xl == 0, pay[2], got_pay[2])
    stats_1 = jnp.where(xl == 0, got_pay[2], pay[2])

    def column(tile, at):
        even, odd = [jnp.sum(jnp.where(l_id == at + p, tile, 0.0), -1, keepdims=True) for p in (0, 2)]
        return jnp.where(l_id < 64, even, odd)

    m_id = lax.broadcasted_iota(jnp.int32, (16, 128), 0)
    for s in range(2):
        gap = (column(stats_0, s * 4) - column(stats_1, s * 4)) * 0.5
        squares = column(stats_0, s * 4 + 1) + column(stats_1, s * 4 + 1)
        slope_0, slope_1, shift = [
            sums[s * 16 + i : s * 16 + i + 1]
            + sums[s * 16 + 3 + i : s * 16 + 4 + i]
            + sums[s * 16 + 6 + i : s * 16 + 7 + i]
            for i in range(3)
        ]
        inverse = lax.rsqrt(squares * (1.0 / D) + gap * gap + 1e-06)
        velocity = inverse * ((pay[s] + got_pay[s]) + gap * (slope_0 - slope_1)) + shift
        row_live = jnp.where(rows < heights[s], 1, 0)
        alive = m_id * 2 + l_id // 64 < widths[s] * row_live
        velocity = jnp.where(alive, velocity, 0.0)
        for m in range(16):
            vel_out[s, :, m * 128 : (m + 1) * 128] = velocity[m : m + 1]

    for copy in q_copies + l_copies + o_copies + a_copies + [b_copy, f_copy]:
        copy.wait_send()
    qs.close()
    ws.close()


def body(
    latents,
    heights,
    widths,
    slot_item,
    step_index,
    cond_table,
    text_kv,
    patch_weight,
    qkv_weight,
    out_weight,
    final_weight,
):
    constants = tables()
    vmem = pl.BlockSpec(memory_space=pltpu.VMEM)
    dma = pltpu.SemaphoreType.DMA
    shape = jax.ShapeDtypeStruct((2, 1, 2048), F32)
    velocity = pl.pallas_call(
        kernel,
        out_shape=shape,
        in_specs=[pl.BlockSpec(memory_space=pl.ANY)] * 18,
        out_specs=vmem,
        scratch_shapes=[
            pltpu.SMEM((2,), jnp.int32),
            pltpu.SMEM((2,), jnp.int32),
            pltpu.SMEM((2,), jnp.int32),
            pltpu.VMEM((2, 16, 128), F32),
            pltpu.VMEM((5, 16, D), F32),
            pltpu.VMEM((154, 2, 384), BF16),
            pltpu.VMEM((64, D), BF16),
            pltpu.VMEM((64, D), BF16),
            pltpu.VMEM((3, 6, 384), BF16),
            pltpu.VMEM((6, 384), BF16),
            pltpu.VMEM((1, D), jnp.int32),
            pltpu.VMEM((480, 1), jnp.int32),
            pltpu.VMEM((32, 1, D), F32),
            pltpu.VMEM((2, 16, D), F32),
            pltpu.VMEM((1, D // 2), jnp.int32),
            pltpu.VMEM((144, 1), jnp.int32),
            pltpu.VMEM((32, 1, D // 2), F32),
            pltpu.VMEM((2, 16, D // 2), F32),
            pltpu.VMEM((2, 16, 128), BF16),
            pltpu.VMEM((2, 32, 128), BF16),
            pltpu.VMEM((2, 16, 128), BF16),
            pltpu.VMEM((3, 32, 128), F32),
            pltpu.VMEM((32, 16, 128), BF16),
            pltpu.VMEM((16, 32, 128), BF16),
            pltpu.VMEM((32, 16, 128), BF16),
            pltpu.VMEM((16, UR, 640), BF16),
            pltpu.VMEM((16, UR // 2, 768), BF16),
            pltpu.VMEM((1024, D), BF16),
            pltpu.VMEM((1024, 384), BF16),
            pltpu.VMEM((2, 128, D), BF16),
            pltpu.VMEM((2, 128, D // 2), BF16),
            pltpu.VMEM((2, 128, D // 2), BF16),
            pltpu.VMEM((16, D), F32),
            pltpu.VMEM((16, D // 2), F32),
            pltpu.VMEM((48, D), F32),
            pltpu.VMEM((32, D), F32),
            pltpu.VMEM((176, D), BF16),
            pltpu.VMEM((112, D), F32),
            pltpu.VMEM((176, D // 2), F32),
            pltpu.VMEM((480, 512), BF16),
            pltpu.VMEM((144, 256), BF16),
            pltpu.VMEM((4, 32, 384), BF16),
            pltpu.VMEM((2, 4, 32, 384), BF16),
            pltpu.VMEM((3, 16, 128), F32),
            pltpu.VMEM((3, 16, 128), F32),
        ]
        + [dma((n,)) for n in (18, 16, 16, 16, 16, 32, 32, 8, 8, 8, 8, 8, 8, 8, 8, 8, 8, 1, 1, 1, 1)],
        compiler_params=pltpu.CompilerParams(
            collective_id=0, has_side_effects=True, vmem_limit_bytes=56 * 1024 * 1024
        ),
    )(
        heights,
        widths,
        slot_item,
        latents.reshape(2, 16, 128),
        cond_table.transpose(1, 0, 2),
        text_kv.transpose(0, 2, 1, 3),
        patch_weight,
        final_weight.T,
        qkv_weight,
        out_weight.T,
        *[jnp.asarray(constant) for constant in constants],
    )
    position = step_index[0].astype(F32)
    sigma_now = sigma_level(position)
    sigma_next = sigma_level(position + 1.0)
    return latents + (sigma_next - sigma_now) * velocity, latents - sigma_now * velocity


def solution(mesh):
    return jax.shard_map(
        body,
        mesh=mesh,
        in_specs=(
            P("item", "rows", None),
            P("item"),
            P("item"),
            P("item"),
            P(),
            P(),
            P("item", None, None, "hid"),
            P(),
            P(None, ("item", "rows"), "hid"),
            P("hid", ("item", "rows")),
            P(),
        ),
        out_specs=(P("item", "rows", None), P("item", "rows", None)),
        check_vma=False,
    )
```

```python
import functools

import jax
import jax.numpy as jnp
import numpy as np
from jax import lax
from jax.experimental import pallas as pl
from jax.experimental.pallas import tpu as pltpu
from jax.sharding import PartitionSpec as P

MESH = pl.DeviceIdType.MESH
HD = 64
STEPS = 28
D = 1536
NY, NZ = 8, 8
UR = 96
F32, BF16 = jnp.float32, jnp.bfloat16


def feature_order():
    order = np.zeros((D,), np.int32)
    at = 0
    for core in range(2):
        for outer in range(8):
            for inner in range(8):
                y, z = (outer, inner) if core == 0 else (inner, outer)
                for xh in range(2):
                    block = y * 32 + z * 4 + xh * 2 + core
                    order[at : at + 6] = 6 * block + np.arange(6)
                    at += 6
    return order


def tables():
    order = feature_order()
    quarter = D // 4
    frequency = (
        np.float32(1.0) / np.float32(10000.0) ** (np.arange(quarter, dtype=np.float32) / np.float32(quarter))
    ).astype(np.float32)
    angle = np.arange(32, dtype=np.float32)[:, None] * frequency[None, :]
    part = np.concatenate([np.sin(angle.astype(np.float64)), np.cos(angle.astype(np.float64))], 1)
    zero = np.zeros_like(part)
    row_table = np.concatenate([part, zero], 1)[:, order].astype(np.float32)
    col_table = np.concatenate([zero, part], 1)[:, order].astype(np.float32)
    pick = np.zeros((480, 1), np.int32)
    for tile in range(5):
        for source in range(16):
            for j in range(6):
                pick[tile * 96 + source * 6 + j, 0] = source * 32 + tile * 6 + j
    pick_out = np.zeros((144, 1), np.int32)
    for tile in range(3):
        for source in range(16):
            for j in range(3):
                pick_out[tile * 48 + source * 3 + j, 0] = source * 16 + tile * 3 + j
    col_table = np.stack([col_table[0::2], col_table[1::2]])
    place = np.arange(D).reshape(256, 2, 3)
    halves = np.stack([place[:, h].reshape(-1) for h in range(2)])
    return (
        order[None, :],
        pick,
        row_table[:, None, :],
        col_table,
        order[halves][:, None, :],
        pick_out,
        np.stack([row_table[:, None, half] for half in halves]),
        np.stack([col_table[:, :, half] for half in halves]),
    )


def sigma_level(position):
    fraction = 1.0 - position / STEPS
    return 3.0 * fraction / (1.0 + 2.0 * fraction)


def relative_partners():
    found = set()
    for dy in range(NY):
        for dz in range(NZ):
            for dxh in range(2):
                for dc in range(2):
                    for dxl in range(2):
                        near = (dy == 0 and dxl == 0 and dxh == 0) or (dy == 0 and dz == 0)
                        near = near or (dc == 0 and (dy == 0 or dz == 0))
                        if near:
                            found.add((dy, dz, dxh, dc, dxl))
    found.discard((0, 0, 0, 0, 0))
    return sorted(found)


def kernel(
    heights_in,
    widths_in,
    slot_in,
    lat_in,
    cond_in,
    text_in,
    wp_in,
    wft_in,
    wq_in,
    wo_in,
    order_in,
    pick_in,
    rowtab_in,
    coltab_in,
    order_h_in,
    pick_o_in,
    rowtab_h_in,
    coltab_h_in,
    vel_out,
    heights,
    widths,
    slot_item,
    lat,
    cond,
    text,
    wp,
    wft,
    wq,
    wo,
    order,
    pick,
    rowtab,
    coltab,
    order_h,
    pick_o,
    rowtab_h,
    coltab_h,
    latb,
    qpiece,
    opiece,
    piece,
    lb,
    qb,
    ob,
    qu,
    ou,
    nb,
    kvb,
    wps,
    wph,
    wfh,
    cperm,
    chalf,
    split,
    sums_in,
    rows_in,
    rows_out,
    rows_half,
    eb,
    eo,
    send_att,
    recv_att,
    pay,
    got_pay,
    sem_in,
    sem_ls,
    sem_lr,
    sem_qs,
    sem_qr,
    sem_os,
    sem_or,
    sem_us,
    sem_ur,
    sem_ps,
    sem_pr,
    sem_ws,
    sem_wr,
    sem_xs,
    sem_xr,
    sem_as,
    sem_ar,
    sem_bs,
    sem_br,
    sem_fs,
    sem_fr,
):
    y = lax.axis_index("item")
    rows = lax.axis_index("rows")
    xl = lax.axis_index("hid")
    z = rows // 4
    xh = (rows // 2) % 2
    core = rows % 2
    by_b = z * (1 - core) + y * core
    by_c = y * (1 - core) + z * core

    def flip(bit, change):
        return bit if change == 0 else 1 - bit

    def device(ty, tz, txh, tc, txl):
        return (ty, tz * 4 + txh * 2 + tc, txl)

    def ring_b(k):
        return (y + core * k) % 8, (z + (1 - core) * k) % 8

    def ring_c(k):
        return (y + (1 - core) * k) % 8, (z + core * k) % 8

    barrier = pltpu.get_barrier_semaphore()
    partners = relative_partners()
    for dy, dz, dxh, dc, dxl in partners:
        pl.semaphore_signal(
            barrier,
            inc=1,
            device_id=device((y + dy) % 8, (z + dz) % 8, flip(xh, dxh), flip(core, dc), flip(xl, dxl)),
            device_id_type=MESH,
        )
    pairs = (
        (wq_in, wq),
        (wo_in, wo),
        (lat_in, lat),
        (wp_in, wp),
        (wft_in, wft),
        (order_in, order),
        (pick_in, pick),
        (cond_in, cond),
        (rowtab_in, rowtab),
        (coltab_in, coltab),
        (text_in.at[core], text),
        (order_h_in.at[xl], order_h),
        (pick_o_in, pick_o),
        (rowtab_h_in.at[xl], rowtab_h),
        (coltab_h_in.at[xl], coltab_h),
        (heights_in, heights),
        (widths_in, widths),
        (slot_in, slot_item),
    )
    loads = [pltpu.make_async_copy(a, b, sem_in.at[i]) for i, (a, b) in enumerate(pairs)]
    for load in loads:
        load.start()
    loads[0].wait()
    for q in range(2):
        cut = slice(q * 192, (q + 1) * 192)
        parts = [wq[i].astype(F32)[:, cut] for i in (1, 2, 0)]
        full = jnp.concatenate(parts + [jnp.zeros((6, 64), F32)], 1)
        for t in range(5):
            piece[q, t * 6 : t * 6 + 6] = full[:, t * 128 : (t + 1) * 128]
        piece[q, 30:32] = jnp.zeros((2, 128), F32)
        qpiece[q] = piece[q].astype(BF16)
    loads[1].wait()
    for half in range(2):
        for t in range(3):
            at = half * 16 + t * 3
            piece[2, at : at + 3] = wo[...].astype(F32)[half * 3 : half * 3 + 3, t * 128 : (t + 1) * 128]
        piece[2, half * 16 + 9 : half * 16 + 16] = jnp.zeros((7, 128), F32)
        opiece[half] = piece[2, half * 16 : half * 16 + 16].astype(BF16)
    loads[2].wait()
    latb[...] = lat[...].astype(BF16)
    my_lat = xh * 16 + z * 2 + core
    lb[my_lat] = latb[core]
    qb[by_b * 2 + xh] = qpiece[xh]
    ob[xl * 16 + by_b * 2 + xh] = opiece[xl]
    pl.semaphore_wait(barrier, len(partners))

    def remote(src, dst, s_sem, r_sem, to):
        return pltpu.make_async_remote_copy(
            src_ref=src, dst_ref=dst, send_sem=s_sem, recv_sem=r_sem, device_id=to, device_id_type=MESH
        )

    q_copies, l_copies, o_copies = [], [], []
    for k in range(8):
        for dxh in range(2):
            if k == 0 and dxh == 0:
                continue
            ty, tz = ring_b(k)
            txh = flip(xh, dxh)
            n = k * 2 + dxh
            q_copies.append(
                remote(
                    qpiece.at[txh],
                    qb.at[by_b * 2 + xh],
                    sem_qs.at[n],
                    sem_qr.at[n],
                    device(ty, tz, txh, core, xl),
                )
            )
            q_copies[-1].start()
    for dz in range(8):
        for dc in range(2):
            n = dz * 2 + dc
            if n == 0:
                continue
            tc = flip(core, dc)
            l_copies.append(
                remote(
                    latb.at[tc],
                    lb.at[my_lat],
                    sem_ls.at[n],
                    sem_lr.at[n],
                    device(y, (z + dz) % 8, xh, tc, xl),
                )
            )
            l_copies[-1].start()
    for load in loads[3:]:
        load.wait()
    eb[...] = (lax.broadcasted_iota(jnp.int32, (480, 512), 1) == pick[...]).astype(F32).astype(BF16)
    eo[...] = (lax.broadcasted_iota(jnp.int32, (144, 256), 1) == pick_o[...]).astype(F32).astype(BF16)

    for copy in q_copies:
        copy.wait_recv()
    packed = jnp.dot(eb[...], qb[...].reshape(512, 128), preferred_element_type=F32).astype(BF16)
    mine = core * 8 + by_c
    for t in range(5):
        qu[mine, :, t * 128 : (t + 1) * 128] = packed[t * 96 : (t + 1) * 96]

    def unit(step):
        return core * 8 + (by_c + step + 8) % 8

    class Spread:
        def __init__(self, buf, s_sem, r_sem, ps_sem, pr_sem):
            self.buf, self.s, self.r, self.ps, self.pr = buf, s_sem, r_sem, ps_sem, pr_sem
            self.cut = buf.shape[1] // 32 * 16 + buf.shape[1] % 32
            self.sent, self.come = [], {}
            self.partner = []

        def send(self, n, origin, step, part=slice(None)):
            ty, tz = ring_c((step + 8) % 8)
            block = self.buf.at[unit(origin), part]
            c = remote(
                block,
                block,
                self.s.at[n],
                self.r.at[n],
                device(ty, tz, xh, core, xl),
            )
            c.start()
            self.sent.append(c)
            self.come[n] = c

        def share(self, n, origin):
            slot = unit(origin)
            c = remote(
                self.buf.at[slot],
                self.buf.at[slot],
                self.ps.at[n],
                self.pr.at[n],
                device(y, z, xh, 1 - core, xl),
            )
            c.start()
            self.partner.append(c)

        def first(self):
            self.send(0, 0, 2)
            self.send(1, 0, -2)
            self.send(2, 0, 1)
            self.send(3, 0, -1)
            self.share(0, 0)

        def second(self):
            self.come[0].wait_recv()
            self.send(4, -2, 1)
            self.send(6, -2, 2, slice(0, self.cut))
            self.come[1].wait_recv()
            self.send(5, 2, -1)
            self.send(7, 2, -2, slice(self.cut, None))
            self.share(1, -2)
            self.share(2, 2)
            self.come[2].wait_recv()
            self.share(3, -1)
            self.come[3].wait_recv()
            self.share(4, 1)

        def third(self):
            self.come[4].wait_recv()
            self.share(5, -3)
            self.come[5].wait_recv()
            self.share(6, 3)
            self.come[6].wait_recv()
            self.come[7].wait_recv()
            self.share(7, -4)

        def last(self):
            for c in self.partner:
                c.wait_recv()

        def close(self):
            for c in self.sent + self.partner:
                c.wait_send()

    qs = Spread(qu, sem_us, sem_ur, sem_ps, sem_pr)
    qs.first()
    for k in range(8):
        for dxh in range(2):
            for dxl in range(2):
                n = k * 4 + dxh * 2 + dxl
                if n == 0:
                    continue
                ty, tz = ring_b(k)
                o_copies.append(
                    remote(
                        opiece.at[flip(xl, dxl)],
                        ob.at[xl * 16 + by_b * 2 + xh],
                        sem_os.at[n],
                        sem_or.at[n],
                        device(ty, tz, flip(xh, dxh), core, flip(xl, dxl)),
                    )
                )
                o_copies[-1].start()


    for copy in l_copies:
        copy.wait_recv()
    block = lb.at[pl.ds(pl.multiple_of(xh * 16, 16), 16)]
    b_copy = remote(block, block, sem_bs.at[0], sem_br.at[0], device(y, z, 1 - xh, core, xl))
    b_copy.start()

    rows_in[0:64] = wp[...]
    rows_in[112:176] = wft[...]

    def three(value):
        hi = value.astype(BF16).astype(F32)
        mid = (value - hi).astype(BF16).astype(F32)
        return hi, mid, (value - hi - mid).astype(BF16).astype(F32)

    in_first = (lax.broadcasted_iota(jnp.int32, (1, D), 1) % 6) < 3
    for s in range(2):
        c = jnp.concatenate([cond[i, pl.ds(slot_item[s], 1)] for i in range(5)], 0)
        for i, part in enumerate(three(c)):
            at = s * 24 + i * 8
            split[at : at + 8] = jnp.concatenate([part, jnp.zeros((3, D), F32)], 0)
        scale_f = 1.0 + c[4:5]
        first = jnp.where(in_first, scale_f, 0.0)
        three_rows = jnp.concatenate([first, scale_f - first, c[3:4]], 0)
        parts = three(three_rows)
        sums_in[s * 16 : s * 16 + 16] = jnp.concatenate(list(parts) + [jnp.zeros((7, D), F32)], 0)
    rows_in[64:112] = split[...].astype(BF16)

    def onehot(names):
        return (lax.broadcasted_iota(jnp.int32, (D, 256), 0) == names).astype(F32).astype(BF16)

    for i in range(6):
        cols = slice(i * 256, (i + 1) * 256)
        rows_out[:, cols] = jnp.dot(rows_in[0:112], onehot(order[:, cols]), preferred_element_type=F32)
    for i in range(3):
        cols = slice(i * 256, (i + 1) * 256)
        rows_half[:, cols] = jnp.dot(rows_in[...], onehot(order_h[:, cols]), preferred_element_type=F32)
    for at, rest in ((0, 64), (1, 0)):
        wps[at, at * 64 : at * 64 + 64] = rows_out[0:64].astype(BF16)
        wps[at, rest : rest + 64] = jnp.zeros((64, D), BF16)
        wph[at, at * 64 : at * 64 + 64] = rows_half[0:64].astype(BF16)
        wph[at, rest : rest + 64] = jnp.zeros((64, D // 2), BF16)
        wfh[at, at * 64 : at * 64 + 64] = rows_half[112:176].astype(BF16)
        wfh[at, rest : rest + 64] = jnp.zeros((64, D // 2), BF16)
    for s in range(2):
        at = 64 + s * 24
        for src, dst in ((rows_out, cperm), (rows_half, chalf)):
            dst[s * 8 : s * 8 + 8] = src[at : at + 8] + src[at + 8 : at + 16] + src[at + 16 : at + 24]
    nt = (((1,), (1,)), ((), ()))
    final_rows = jnp.concatenate([wft[...], wft[...]], 0)
    sums = lax.dot_general(sums_in[...].astype(BF16), final_rows, nt, preferred_element_type=F32)

    r_id = lax.broadcasted_iota(jnp.int32, (384, 384), 0)
    c_id = lax.broadcasted_iota(jnp.int32, (384, 384), 1)
    pick_key = ((r_id == c_id + 192 * xh) & (c_id < 192)).astype(F32).astype(BF16)
    pick_val = ((r_id == c_id - 192 + 192 * xh) & (c_id >= 192)).astype(F32).astype(BF16)
    place = ((r_id - 64 + 192 * xh == c_id) & (r_id >= 64)).astype(F32).astype(BF16)[0:256]
    text_rows = (
        jnp.dot(text[:, 0], pick_key, preferred_element_type=F32)
        + jnp.dot(text[:, 1], pick_val, preferred_element_type=F32)
    ).astype(BF16)

    def normalise(value):
        mean = jnp.mean(value, -1, keepdims=True)
        centered = value - mean
        return centered * lax.rsqrt(jnp.mean(centered * centered, -1, keepdims=True) + 1e-06)

    cmine = cperm[pl.ds(pl.multiple_of(core * 8, 8), 8)]
    shift_a, scale_a = cmine[0:1], 1.0 + cmine[1:2]

    def norm_half(half):
        def chunk(i, carry):
            x = lb[pl.ds(half * 16 + i * 4, 4)].reshape(64, 128)
            for parity in range(2):
                e = jnp.dot(x, wps[parity], preferred_element_type=F32)
                for rr in range(4):
                    row = (i * 2 + rr // 2) * 4 + half * 2 + rr % 2
                    part = e[rr * 16 : rr * 16 + 16] + (rowtab[row] + coltab[parity])
                    at = (row // 4) * 128 + parity * 64 + (row % 4) * 16
                    nb[pl.ds(pl.multiple_of(at, 16), 16)] = (normalise(part) * scale_a + shift_a).astype(BF16)
            return carry

        lax.fori_loop(0, 4, chunk, 0)

    norm_half(xh)
    qs.second()
    for copy in o_copies:
        copy.wait_recv()
    for half in range(2):
        got = jnp.dot(
            eo[...], ob[half * 16 : half * 16 + 16].reshape(256, 128), preferred_element_type=F32
        ).astype(BF16)
        for t in range(3):
            ou[mine, :, half * 384 + t * 128 : half * 384 + (t + 1) * 128] = got[t * 48 : (t + 1) * 48]
    ws = Spread(ou, sem_ws, sem_wr, sem_xs, sem_xr)
    ws.first()
    b_copy.wait_recv()
    norm_half(1 - xh)
    qs.third()
    qs.last()

    kvb[...] = jnp.dot(nb[...], qu[:, :, 0:384].reshape(D, 384), preferred_element_type=F32).astype(BF16)
    queries = jnp.dot(
        nb[pl.ds(pl.multiple_of(z * 128, 128), 128)],
        qu[:, :, 384:640].reshape(D, 256),
        preferred_element_type=F32,
    ).astype(BF16)
    ws.second()

    height, width = heights[core], widths[core]
    key_id = lax.broadcasted_iota(jnp.int32, (1, 1024), 1)
    key_row = (key_id // 128) * 4 + (key_id // 16) % 4
    key_col = (key_id % 16) * 2 + (key_id // 64) % 2
    live = (key_row < height) & (key_col < width)
    lane = lax.broadcasted_iota(jnp.int32, (1, 256), 1)
    keys, values = kvb[:, 0:256], kvb[:, 128:384]
    attended = jnp.zeros((128, 256), F32)
    masked = [
        jnp.where((lane >= 64 * h) & (lane < 64 * h + 64), queries.astype(F32) * HD ** (-0.5), 0.0).astype(BF16) for h in range(3)
    ]
    stacked = jnp.concatenate(masked, 0)
    s_text = lax.dot_general(stacked, text_rows[:, 0:256], nt, preferred_element_type=F32)
    s_img = lax.dot_general(stacked, keys, nt, preferred_element_type=F32)
    s_img = jnp.where(live, s_img, -1e30)
    top = jnp.maximum(jnp.max(s_text, -1, keepdims=True), jnp.max(s_img, -1, keepdims=True))
    w_text = jnp.exp(s_text - top)
    w_img = jnp.exp(s_img - top)
    total = jnp.sum(w_text, -1, keepdims=True) + jnp.sum(w_img, -1, keepdims=True)
    acc = jnp.dot(w_text.astype(BF16), text_rows[:, 128:384], preferred_element_type=F32) + jnp.dot(
        w_img.astype(BF16), values, preferred_element_type=F32
    )
    acc = acc * (1.0 / total)
    for h in range(3):
        inside = (lane >= 64 + 64 * h) & (lane < 128 + 64 * h)
        attended = attended + jnp.where(inside, acc[h * 128 : (h + 1) * 128], 0.0)
    placed = jnp.dot(attended.astype(BF16), place, preferred_element_type=F32).astype(BF16)
    for j in range(4):
        for parity in range(2):
            send_att[j, parity * 16 : parity * 16 + 16] = placed[
                parity * 64 + j * 16 : parity * 64 + j * 16 + 16
            ]
    head_at = xl * 2 + xh
    a_copies = []
    for n in range(1, 8):
        txh, tc, txl = flip(xh, n // 4), flip(core, (n // 2) % 2), flip(xl, n % 2)
        a_copies.append(
            remote(
                send_att.at[txh * 2 + tc],
                recv_att.at[core, head_at],
                sem_as.at[n],
                sem_ar.at[n],
                device(y, z, txh, tc, txl),
            )
        )
        a_copies[-1].start()
    recv_att[core, head_at] = send_att[xh * 2 + core]
    ws.third()
    ws.last()
    for copy in a_copies:
        copy.wait_recv()

    halves = [
        jnp.concatenate([recv_att[s, 2 * g] + recv_att[s, 2 * g + 1] for s in range(2)], 0) for g in range(2)
    ]
    projected = lax.dot_general(
        jnp.concatenate(halves, 1), ou[...].reshape(D // 2, 768), nt, preferred_element_type=F32
    )
    l_id = lax.broadcasted_iota(jnp.int32, (16, 128), 1)
    stats = jnp.zeros((16, 128), F32)
    for s in range(2):
        gate = chalf[s * 8 + 2 : s * 8 + 3]
        scale_f = 1.0 + chalf[s * 8 + 4 : s * 8 + 5]
        product = jnp.zeros((16, 128), F32)
        for parity in range(2):
            e = jnp.dot(latb[s], wph[parity], preferred_element_type=F32) + (rowtab_h[rows] + coltab_h[parity])
            at = s * 32 + parity * 16
            residual = e + gate * projected[at : at + 16]
            mean = jnp.mean(residual, -1, keepdims=True)
            centered = residual - mean
            squares = jnp.sum(centered * centered, -1, keepdims=True)
            stats = jnp.where(l_id == s * 4 + parity * 2, mean, stats)
            stats = jnp.where(l_id == s * 4 + parity * 2 + 1, squares, stats)
            product = product + lax.dot_general(
                (centered * scale_f).astype(BF16), wfh[parity], nt, preferred_element_type=F32
            )
        pay[s] = product
    pay[2] = stats
    f_copy = remote(pay, got_pay, sem_fs.at[0], sem_fr.at[0], device(y, z, xh, core, 1 - xl))
    f_copy.start()
    f_copy.wait_recv()
    stats_0 = jnp.where(xl == 0, pay[2], got_pay[2])
    stats_1 = jnp.where(xl == 0, got_pay[2], pay[2])

    def column(tile, at):
        even, odd = [jnp.sum(jnp.where(l_id == at + p, tile, 0.0), -1, keepdims=True) for p in (0, 2)]
        return jnp.where(l_id < 64, even, odd)

    m_id = lax.broadcasted_iota(jnp.int32, (16, 128), 0)
    for s in range(2):
        gap = (column(stats_0, s * 4) - column(stats_1, s * 4)) * 0.5
        squares = column(stats_0, s * 4 + 1) + column(stats_1, s * 4 + 1)
        slope_0, slope_1, shift = [
            sums[s * 16 + i : s * 16 + i + 1]
            + sums[s * 16 + 3 + i : s * 16 + 4 + i]
            + sums[s * 16 + 6 + i : s * 16 + 7 + i]
            for i in range(3)
        ]
        inverse = lax.rsqrt(squares * (1.0 / D) + gap * gap + 1e-06)
        velocity = inverse * ((pay[s] + got_pay[s]) + gap * (slope_0 - slope_1)) + shift
        row_live = jnp.where(rows < heights[s], 1, 0)
        alive = m_id * 2 + l_id // 64 < widths[s] * row_live
        velocity = jnp.where(alive, velocity, 0.0)
        for m in range(16):
            vel_out[s, :, m * 128 : (m + 1) * 128] = velocity[m : m + 1]

    for copy in q_copies + l_copies + o_copies + a_copies + [b_copy, f_copy]:
        copy.wait_send()
    qs.close()
    ws.close()


def body(
    latents,
    heights,
    widths,
    slot_item,
    step_index,
    cond_table,
    text_kv,
    patch_weight,
    qkv_weight,
    out_weight,
    final_weight,
):
    constants = tables()
    vmem = pl.BlockSpec(memory_space=pltpu.VMEM)
    dma = pltpu.SemaphoreType.DMA
    shape = jax.ShapeDtypeStruct((2, 1, 2048), F32)
    velocity = pl.pallas_call(
        kernel,
        out_shape=shape,
        in_specs=[pl.BlockSpec(memory_space=pl.ANY)] * 18,
        out_specs=vmem,
        scratch_shapes=[
            pltpu.SMEM((2,), jnp.int32),
            pltpu.SMEM((2,), jnp.int32),
            pltpu.SMEM((2,), jnp.int32),
            pltpu.VMEM((2, 16, 128), F32),
            pltpu.VMEM((5, 16, D), F32),
            pltpu.VMEM((154, 2, 384), BF16),
            pltpu.VMEM((64, D), BF16),
            pltpu.VMEM((64, D), BF16),
            pltpu.VMEM((3, 6, 384), BF16),
            pltpu.VMEM((6, 384), BF16),
            pltpu.VMEM((1, D), jnp.int32),
            pltpu.VMEM((480, 1), jnp.int32),
            pltpu.VMEM((32, 1, D), F32),
            pltpu.VMEM((2, 16, D), F32),
            pltpu.VMEM((1, D // 2), jnp.int32),
            pltpu.VMEM((144, 1), jnp.int32),
            pltpu.VMEM((32, 1, D // 2), F32),
            pltpu.VMEM((2, 16, D // 2), F32),
            pltpu.VMEM((2, 16, 128), BF16),
            pltpu.VMEM((2, 32, 128), BF16),
            pltpu.VMEM((2, 16, 128), BF16),
            pltpu.VMEM((3, 32, 128), F32),
            pltpu.VMEM((32, 16, 128), BF16),
            pltpu.VMEM((16, 32, 128), BF16),
            pltpu.VMEM((32, 16, 128), BF16),
            pltpu.VMEM((16, UR, 640), BF16),
            pltpu.VMEM((16, UR // 2, 768), BF16),
            pltpu.VMEM((1024, D), BF16),
            pltpu.VMEM((1024, 384), BF16),
            pltpu.VMEM((2, 128, D), BF16),
            pltpu.VMEM((2, 128, D // 2), BF16),
            pltpu.VMEM((2, 128, D // 2), BF16),
            pltpu.VMEM((16, D), F32),
            pltpu.VMEM((16, D // 2), F32),
            pltpu.VMEM((48, D), F32),
            pltpu.VMEM((32, D), F32),
            pltpu.VMEM((176, D), BF16),
            pltpu.VMEM((112, D), F32),
            pltpu.VMEM((176, D // 2), F32),
            pltpu.VMEM((480, 512), BF16),
            pltpu.VMEM((144, 256), BF16),
            pltpu.VMEM((4, 32, 384), BF16),
            pltpu.VMEM((2, 4, 32, 384), BF16),
            pltpu.VMEM((3, 16, 128), F32),
            pltpu.VMEM((3, 16, 128), F32),
        ]
        + [dma((n,)) for n in (18, 16, 16, 16, 16, 32, 32, 8, 8, 8, 8, 8, 8, 8, 8, 8, 8, 1, 1, 1, 1)],
        compiler_params=pltpu.CompilerParams(
            collective_id=0, has_side_effects=True, vmem_limit_bytes=56 * 1024 * 1024
        ),
    )(
        heights,
        widths,
        slot_item,
        latents.reshape(2, 16, 128),
        cond_table.transpose(1, 0, 2),
        text_kv.transpose(0, 2, 1, 3),
        patch_weight,
        final_weight.T,
        qkv_weight,
        out_weight.T,
        *[jnp.asarray(constant) for constant in constants],
    )
    position = step_index[0].astype(F32)
    sigma_now = sigma_level(position)
    sigma_next = sigma_level(position + 1.0)
    return latents + (sigma_next - sigma_now) * velocity, latents - sigma_now * velocity


def solution(mesh):
    return jax.shard_map(
        body,
        mesh=mesh,
        in_specs=(
            P("item", "rows", None),
            P("item"),
            P("item"),
            P("item"),
            P(),
            P(),
            P("item", None, None, "hid"),
            P(),
            P(None, ("item", "rows"), "hid"),
            P("hid", ("item", "rows")),
            P(),
        ),
        out_specs=(P("item", "rows", None), P("item", "rows", None)),
        check_vma=False,
    )
```

```python
import functools

import jax
import jax.numpy as jnp
import numpy as np
from jax import lax
from jax.experimental import pallas as pl
from jax.experimental.pallas import tpu as pltpu
from jax.sharding import PartitionSpec as P

MESH = pl.DeviceIdType.MESH
HD = 64
STEPS = 28
D = 1536
NY, NZ = 8, 8
UR = 96
F32, BF16 = jnp.float32, jnp.bfloat16


def feature_order():
    order = np.zeros((D,), np.int32)
    at = 0
    for core in range(2):
        for outer in range(8):
            for inner in range(8):
                y, z = (outer, inner) if core == 0 else (inner, outer)
                for xh in range(2):
                    block = y * 32 + z * 4 + xh * 2 + core
                    order[at : at + 6] = 6 * block + np.arange(6)
                    at += 6
    return order


def tables():
    order = feature_order()
    quarter = D // 4
    frequency = (
        np.float32(1.0) / np.float32(10000.0) ** (np.arange(quarter, dtype=np.float32) / np.float32(quarter))
    ).astype(np.float32)
    angle = np.arange(32, dtype=np.float32)[:, None] * frequency[None, :]
    part = np.concatenate([np.sin(angle.astype(np.float64)), np.cos(angle.astype(np.float64))], 1)
    zero = np.zeros_like(part)
    row_table = np.concatenate([part, zero], 1)[:, order].astype(np.float32)
    col_table = np.concatenate([zero, part], 1)[:, order].astype(np.float32)
    pick = np.zeros((480, 1), np.int32)
    for tile in range(5):
        for source in range(16):
            for j in range(6):
                pick[tile * 96 + source * 6 + j, 0] = source * 32 + tile * 6 + j
    pick_out = np.zeros((144, 1), np.int32)
    for tile in range(3):
        for source in range(16):
            for j in range(3):
                pick_out[tile * 48 + source * 3 + j, 0] = source * 16 + tile * 3 + j
    col_table = np.stack([col_table[0::2], col_table[1::2]])
    place = np.arange(D).reshape(256, 2, 3)
    halves = np.stack([place[:, h].reshape(-1) for h in range(2)])
    return (
        order[None, :],
        pick,
        row_table[:, None, :],
        col_table,
        order[halves][:, None, :],
        pick_out,
        np.stack([row_table[:, None, half] for half in halves]),
        np.stack([col_table[:, :, half] for half in halves]),
    )


def sigma_level(position):
    fraction = 1.0 - position / STEPS
    return 3.0 * fraction / (1.0 + 2.0 * fraction)


def relative_partners():
    found = set()
    for dy in range(NY):
        for dz in range(NZ):
            for dxh in range(2):
                for dc in range(2):
                    for dxl in range(2):
                        near = (dy == 0 and dxl == 0 and dxh == 0) or (dy == 0 and dz == 0)
                        near = near or (dc == 0 and (dy == 0 or dz == 0))
                        if near:
                            found.add((dy, dz, dxh, dc, dxl))
    found.discard((0, 0, 0, 0, 0))
    return sorted(found)


def kernel(
    heights_in,
    widths_in,
    slot_in,
    lat_in,
    cond_in,
    text_in,
    wp_in,
    wft_in,
    wq_in,
    wo_in,
    order_in,
    pick_in,
    rowtab_in,
    coltab_in,
    order_h_in,
    pick_o_in,
    rowtab_h_in,
    coltab_h_in,
    vel_out,
    heights,
    widths,
    slot_item,
    lat,
    cond,
    text,
    wp,
    wft,
    wq,
    wo,
    order,
    pick,
    rowtab,
    coltab,
    order_h,
    pick_o,
    rowtab_h,
    coltab_h,
    latb,
    qpiece,
    opiece,
    piece,
    lb,
    qb,
    ob,
    qu,
    ou,
    nb,
    kvb,
    wps,
    wph,
    wfh,
    cperm,
    chalf,
    split,
    sums_in,
    rows_in,
    rows_out,
    rows_half,
    eb,
    eo,
    send_att,
    recv_att,
    pay,
    got_pay,
    sem_in,
    sem_ls,
    sem_lr,
    sem_qs,
    sem_qr,
    sem_os,
    sem_or,
    sem_us,
    sem_ur,
    sem_ps,
    sem_pr,
    sem_ws,
    sem_wr,
    sem_xs,
    sem_xr,
    sem_as,
    sem_ar,
    sem_bs,
    sem_br,
    sem_fs,
    sem_fr,
):
    y = lax.axis_index("item")
    rows = lax.axis_index("rows")
    xl = lax.axis_index("hid")
    z = rows // 4
    xh = (rows // 2) % 2
    core = rows % 2
    by_b = z * (1 - core) + y * core
    by_c = y * (1 - core) + z * core

    def flip(bit, change):
        return bit if change == 0 else 1 - bit

    def device(ty, tz, txh, tc, txl):
        return (ty, tz * 4 + txh * 2 + tc, txl)

    def ring_b(k):
        return (y + core * k) % 8, (z + (1 - core) * k) % 8

    def ring_c(k):
        return (y + (1 - core) * k) % 8, (z + core * k) % 8

    barrier = pltpu.get_barrier_semaphore()
    partners = relative_partners()
    for dy, dz, dxh, dc, dxl in partners:
        pl.semaphore_signal(
            barrier,
            inc=1,
            device_id=device((y + dy) % 8, (z + dz) % 8, flip(xh, dxh), flip(core, dc), flip(xl, dxl)),
            device_id_type=MESH,
        )
    pairs = (
        (wq_in, wq),
        (wo_in, wo),
        (lat_in, lat),
        (wp_in, wp),
        (wft_in, wft),
        (order_in, order),
        (pick_in, pick),
        (cond_in, cond),
        (rowtab_in, rowtab),
        (coltab_in, coltab),
        (text_in.at[core], text),
        (order_h_in.at[xl], order_h),
        (pick_o_in, pick_o),
        (rowtab_h_in.at[xl], rowtab_h),
        (coltab_h_in.at[xl], coltab_h),
        (heights_in, heights),
        (widths_in, widths),
        (slot_in, slot_item),
    )
    loads = [pltpu.make_async_copy(a, b, sem_in.at[i]) for i, (a, b) in enumerate(pairs)]
    for load in loads:
        load.start()
    loads[0].wait()
    for q in range(2):
        cut = slice(q * 192, (q + 1) * 192)
        parts = [wq[i].astype(F32)[:, cut] for i in (1, 2, 0)]
        full = jnp.concatenate(parts + [jnp.zeros((6, 64), F32)], 1)
        for t in range(5):
            piece[q, t * 6 : t * 6 + 6] = full[:, t * 128 : (t + 1) * 128]
        piece[q, 30:32] = jnp.zeros((2, 128), F32)
        qpiece[q] = piece[q].astype(BF16)
    loads[1].wait()
    for half in range(2):
        for t in range(3):
            at = half * 16 + t * 3
            piece[2, at : at + 3] = wo[...].astype(F32)[half * 3 : half * 3 + 3, t * 128 : (t + 1) * 128]
        piece[2, half * 16 + 9 : half * 16 + 16] = jnp.zeros((7, 128), F32)
        opiece[half] = piece[2, half * 16 : half * 16 + 16].astype(BF16)
    loads[2].wait()
    latb[...] = lat[...].astype(BF16)
    my_lat = xh * 16 + z * 2 + core
    lb[my_lat] = latb[core]
    qb[by_b * 2 + xh] = qpiece[xh]
    ob[xl * 16 + by_b * 2 + xh] = opiece[xl]
    pl.semaphore_wait(barrier, len(partners))

    def remote(src, dst, s_sem, r_sem, to):
        return pltpu.make_async_remote_copy(
            src_ref=src, dst_ref=dst, send_sem=s_sem, recv_sem=r_sem, device_id=to, device_id_type=MESH
        )

    q_copies, l_copies, o_copies = [], [], []
    for k in range(8):
        for dxh in range(2):
            if k == 0 and dxh == 0:
                continue
            ty, tz = ring_b(k)
            txh = flip(xh, dxh)
            n = k * 2 + dxh
            q_copies.append(
                remote(
                    qpiece.at[txh],
                    qb.at[by_b * 2 + xh],
                    sem_qs.at[n],
                    sem_qr.at[n],
                    device(ty, tz, txh, core, xl),
                )
            )
            q_copies[-1].start()
    for dz in range(8):
        for dc in range(2):
            n = dz * 2 + dc
            if n == 0:
                continue
            tc = flip(core, dc)
            l_copies.append(
                remote(
                    latb.at[tc],
                    lb.at[my_lat],
                    sem_ls.at[n],
                    sem_lr.at[n],
                    device(y, (z + dz) % 8, xh, tc, xl),
                )
            )
            l_copies[-1].start()
    for k in range(8):
        for dxh in range(2):
            for dxl in range(2):
                n = k * 4 + dxh * 2 + dxl
                if n == 0:
                    continue
                ty, tz = ring_b(k)
                o_copies.append(
                    remote(
                        opiece.at[flip(xl, dxl)],
                        ob.at[xl * 16 + by_b * 2 + xh],
                        sem_os.at[n],
                        sem_or.at[n],
                        device(ty, tz, flip(xh, dxh), core, flip(xl, dxl)),
                    )
                )
                o_copies[-1].start()


    for load in loads[3:]:
        load.wait()
    eb[...] = (lax.broadcasted_iota(jnp.int32, (480, 512), 1) == pick[...]).astype(F32).astype(BF16)
    eo[...] = (lax.broadcasted_iota(jnp.int32, (144, 256), 1) == pick_o[...]).astype(F32).astype(BF16)

    for copy in q_copies:
        copy.wait_recv()
    packed = jnp.dot(eb[...], qb[...].reshape(512, 128), preferred_element_type=F32).astype(BF16)
    mine = core * 8 + by_c
    for t in range(5):
        qu[mine, :, t * 128 : (t + 1) * 128] = packed[t * 96 : (t + 1) * 96]

    def unit(step):
        return core * 8 + (by_c + step + 8) % 8

    class Spread:
        def __init__(self, buf, s_sem, r_sem, ps_sem, pr_sem):
            self.buf, self.s, self.r, self.ps, self.pr = buf, s_sem, r_sem, ps_sem, pr_sem
            self.cut = buf.shape[1] // 32 * 16 + buf.shape[1] % 32
            self.sent, self.come = [], {}
            self.partner = []

        def send(self, n, origin, step, part=slice(None)):
            ty, tz = ring_c((step + 8) % 8)
            block = self.buf.at[unit(origin), part]
            c = remote(
                block,
                block,
                self.s.at[n],
                self.r.at[n],
                device(ty, tz, xh, core, xl),
            )
            c.start()
            self.sent.append(c)
            self.come[n] = c

        def share(self, n, origin):
            slot = unit(origin)
            c = remote(
                self.buf.at[slot],
                self.buf.at[slot],
                self.ps.at[n],
                self.pr.at[n],
                device(y, z, xh, 1 - core, xl),
            )
            c.start()
            self.partner.append(c)

        def first(self):
            self.send(0, 0, 2)
            self.send(1, 0, -2)
            self.send(2, 0, 1)
            self.send(3, 0, -1)
            self.share(0, 0)

        def second(self):
            self.come[0].wait_recv()
            self.send(4, -2, 1)
            self.send(6, -2, 2, slice(0, self.cut))
            self.come[1].wait_recv()
            self.send(5, 2, -1)
            self.send(7, 2, -2, slice(self.cut, None))
            self.share(1, -2)
            self.share(2, 2)
            self.come[2].wait_recv()
            self.share(3, -1)
            self.come[3].wait_recv()
            self.share(4, 1)

        def third(self):
            self.come[4].wait_recv()
            self.share(5, -3)
            self.come[5].wait_recv()
            self.share(6, 3)
            self.come[6].wait_recv()
            self.come[7].wait_recv()
            self.share(7, -4)

        def last(self):
            for c in self.partner:
                c.wait_recv()

        def close(self):
            for c in self.sent + self.partner:
                c.wait_send()

    qs = Spread(qu, sem_us, sem_ur, sem_ps, sem_pr)
    qs.first()
    for copy in l_copies:
        copy.wait_recv()
    block = lb.at[pl.ds(pl.multiple_of(xh * 16, 16), 16)]
    b_copy = remote(block, block, sem_bs.at[0], sem_br.at[0], device(y, z, 1 - xh, core, xl))
    b_copy.start()

    rows_in[0:64] = wp[...]
    rows_in[112:176] = wft[...]

    def three(value):
        hi = value.astype(BF16).astype(F32)
        mid = (value - hi).astype(BF16).astype(F32)
        return hi, mid, (value - hi - mid).astype(BF16).astype(F32)

    in_first = (lax.broadcasted_iota(jnp.int32, (1, D), 1) % 6) < 3
    for s in range(2):
        c = jnp.concatenate([cond[i, pl.ds(slot_item[s], 1)] for i in range(5)], 0)
        for i, part in enumerate(three(c)):
            at = s * 24 + i * 8
            split[at : at + 8] = jnp.concatenate([part, jnp.zeros((3, D), F32)], 0)
        scale_f = 1.0 + c[4:5]
        first = jnp.where(in_first, scale_f, 0.0)
        three_rows = jnp.concatenate([first, scale_f - first, c[3:4]], 0)
        parts = three(three_rows)
        sums_in[s * 16 : s * 16 + 16] = jnp.concatenate(list(parts) + [jnp.zeros((7, D), F32)], 0)
    rows_in[64:112] = split[...].astype(BF16)

    def onehot(names):
        return (lax.broadcasted_iota(jnp.int32, (D, 256), 0) == names).astype(F32).astype(BF16)

    for i in range(6):
        cols = slice(i * 256, (i + 1) * 256)
        rows_out[:, cols] = jnp.dot(rows_in[0:112], onehot(order[:, cols]), preferred_element_type=F32)
    for i in range(3):
        cols = slice(i * 256, (i + 1) * 256)
        rows_half[:, cols] = jnp.dot(rows_in[...], onehot(order_h[:, cols]), preferred_element_type=F32)
    for at, rest in ((0, 64), (1, 0)):
        wps[at, at * 64 : at * 64 + 64] = rows_out[0:64].astype(BF16)
        wps[at, rest : rest + 64] = jnp.zeros((64, D), BF16)
        wph[at, at * 64 : at * 64 + 64] = rows_half[0:64].astype(BF16)
        wph[at, rest : rest + 64] = jnp.zeros((64, D // 2), BF16)
        wfh[at, at * 64 : at * 64 + 64] = rows_half[112:176].astype(BF16)
        wfh[at, rest : rest + 64] = jnp.zeros((64, D // 2), BF16)
    for s in range(2):
        at = 64 + s * 24
        for src, dst in ((rows_out, cperm), (rows_half, chalf)):
            dst[s * 8 : s * 8 + 8] = src[at : at + 8] + src[at + 8 : at + 16] + src[at + 16 : at + 24]
    nt = (((1,), (1,)), ((), ()))
    final_rows = jnp.concatenate([wft[...], wft[...]], 0)
    sums = lax.dot_general(sums_in[...].astype(BF16), final_rows, nt, preferred_element_type=F32)

    r_id = lax.broadcasted_iota(jnp.int32, (384, 384), 0)
    c_id = lax.broadcasted_iota(jnp.int32, (384, 384), 1)
    pick_key = ((r_id == c_id + 192 * xh) & (c_id < 192)).astype(F32).astype(BF16)
    pick_val = ((r_id == c_id - 192 + 192 * xh) & (c_id >= 192)).astype(F32).astype(BF16)
    place = [
        ((r_id - 64 + 192 * g == c_id) & (r_id >= 64)).astype(F32).astype(BF16)[0:256] for g in range(2)
    ]
    text_rows = (
        jnp.dot(text[:, 0], pick_key, preferred_element_type=F32)
        + jnp.dot(text[:, 1], pick_val, preferred_element_type=F32)
    ).astype(BF16)

    def normalise(value):
        mean = jnp.mean(value, -1, keepdims=True)
        centered = value - mean
        return centered * lax.rsqrt(jnp.mean(centered * centered, -1, keepdims=True) + 1e-06)

    cmine = cperm[pl.ds(pl.multiple_of(core * 8, 8), 8)]
    shift_a, scale_a = cmine[0:1], 1.0 + cmine[1:2]

    def norm_half(half):
        def chunk(i, carry):
            x = lb[pl.ds(half * 16 + i * 4, 4)].reshape(64, 128)
            for parity in range(2):
                e = jnp.dot(x, wps[parity], preferred_element_type=F32)
                for rr in range(4):
                    row = (i * 2 + rr // 2) * 4 + half * 2 + rr % 2
                    part = e[rr * 16 : rr * 16 + 16] + (rowtab[row] + coltab[parity])
                    at = (row // 4) * 128 + parity * 64 + (row % 4) * 16
                    nb[pl.ds(pl.multiple_of(at, 16), 16)] = (normalise(part) * scale_a + shift_a).astype(BF16)
            return carry

        lax.fori_loop(0, 4, chunk, 0)

    norm_half(xh)
    qs.second()
    for copy in o_copies:
        copy.wait_recv()
    for half in range(2):
        got = jnp.dot(
            eo[...], ob[half * 16 : half * 16 + 16].reshape(256, 128), preferred_element_type=F32
        ).astype(BF16)
        for t in range(3):
            ou[mine, :, half * 384 + t * 128 : half * 384 + (t + 1) * 128] = got[t * 48 : (t + 1) * 48]
    ws = Spread(ou, sem_ws, sem_wr, sem_xs, sem_xr)
    ws.first()
    b_copy.wait_recv()
    norm_half(1 - xh)
    qs.third()
    qs.last()

    kvb[...] = jnp.dot(nb[...], qu[:, :, 0:384].reshape(D, 384), preferred_element_type=F32).astype(BF16)
    queries = jnp.dot(
        nb[pl.ds(pl.multiple_of(z * 128, 128), 128)],
        qu[:, :, 384:640].reshape(D, 256),
        preferred_element_type=F32,
    ).astype(BF16)
    ws.second()

    height, width = heights[core], widths[core]
    key_id = lax.broadcasted_iota(jnp.int32, (1, 1024), 1)
    key_row = (key_id // 128) * 4 + (key_id // 16) % 4
    key_col = (key_id % 16) * 2 + (key_id // 64) % 2
    live = (key_row < height) & (key_col < width)
    lane = lax.broadcasted_iota(jnp.int32, (1, 256), 1)
    keys, values = kvb[:, 0:256], kvb[:, 128:384]
    attended = jnp.zeros((128, 256), F32)
    masked = [
        jnp.where((lane >= 64 * h) & (lane < 64 * h + 64), queries.astype(F32) * HD ** (-0.5), 0.0).astype(BF16) for h in range(3)
    ]
    stacked = jnp.concatenate(masked, 0)
    s_text = lax.dot_general(stacked, text_rows[:, 0:256], nt, preferred_element_type=F32)
    s_img = lax.dot_general(stacked, keys, nt, preferred_element_type=F32)
    s_img = jnp.where(live, s_img, -1e30)
    top = jnp.maximum(jnp.max(s_text, -1, keepdims=True), jnp.max(s_img, -1, keepdims=True))
    w_text = jnp.exp(s_text - top)
    w_img = jnp.exp(s_img - top)
    total = jnp.sum(w_text, -1, keepdims=True) + jnp.sum(w_img, -1, keepdims=True)
    acc = jnp.dot(w_text.astype(BF16), text_rows[:, 128:384], preferred_element_type=F32) + jnp.dot(
        w_img.astype(BF16), values, preferred_element_type=F32
    )
    acc = acc * (1.0 / total)
    for h in range(3):
        inside = (lane >= 64 + 64 * h) & (lane < 128 + 64 * h)
        attended = attended + jnp.where(inside, acc[h * 128 : (h + 1) * 128], 0.0)
    placed = attended.astype(BF16)
    for j in range(4):
        for parity in range(2):
            send_att[j, parity * 16 : parity * 16 + 16] = placed[
                parity * 64 + j * 16 : parity * 64 + j * 16 + 16
            ]
    head_at = xl * 2 + xh
    a_copies = []
    for n in range(1, 8):
        txh, tc, txl = flip(xh, n // 4), flip(core, (n // 2) % 2), flip(xl, n % 2)
        a_copies.append(
            remote(
                send_att.at[txh * 2 + tc],
                recv_att.at[core, head_at],
                sem_as.at[n],
                sem_ar.at[n],
                device(y, z, txh, tc, txl),
            )
        )
        a_copies[-1].start()
    recv_att[core, head_at] = send_att[xh * 2 + core]
    ws.third()
    ws.last()
    for copy in a_copies:
        copy.wait_recv()

    halves = []
    for g in range(2):
        sides = [jnp.concatenate([recv_att[s, 2 * g + side] for s in range(2)], 0) for side in range(2)]
        halves.append(
            (
                jnp.dot(sides[0], place[0], preferred_element_type=F32)
                + jnp.dot(sides[1], place[1], preferred_element_type=F32)
            ).astype(BF16)
        )
    projected = lax.dot_general(
        jnp.concatenate(halves, 1), ou[...].reshape(D // 2, 768), nt, preferred_element_type=F32
    )
    l_id = lax.broadcasted_iota(jnp.int32, (16, 128), 1)
    stats = jnp.zeros((16, 128), F32)
    for s in range(2):
        gate = chalf[s * 8 + 2 : s * 8 + 3]
        scale_f = 1.0 + chalf[s * 8 + 4 : s * 8 + 5]
        product = jnp.zeros((16, 128), F32)
        for parity in range(2):
            e = jnp.dot(latb[s], wph[parity], preferred_element_type=F32) + (rowtab_h[rows] + coltab_h[parity])
            at = s * 32 + parity * 16
            residual = e + gate * projected[at : at + 16]
            mean = jnp.mean(residual, -1, keepdims=True)
            centered = residual - mean
            squares = jnp.sum(centered * centered, -1, keepdims=True)
            stats = jnp.where(l_id == s * 4 + parity * 2, mean, stats)
            stats = jnp.where(l_id == s * 4 + parity * 2 + 1, squares, stats)
            product = product + lax.dot_general(
                (centered * scale_f).astype(BF16), wfh[parity], nt, preferred_element_type=F32
            )
        pay[s] = product
    pay[2] = stats
    f_copy = remote(pay, got_pay, sem_fs.at[0], sem_fr.at[0], device(y, z, xh, core, 1 - xl))
    f_copy.start()
    f_copy.wait_recv()
    stats_0 = jnp.where(xl == 0, pay[2], got_pay[2])
    stats_1 = jnp.where(xl == 0, got_pay[2], pay[2])

    def column(tile, at):
        even, odd = [jnp.sum(jnp.where(l_id == at + p, tile, 0.0), -1, keepdims=True) for p in (0, 2)]
        return jnp.where(l_id < 64, even, odd)

    m_id = lax.broadcasted_iota(jnp.int32, (16, 128), 0)
    for s in range(2):
        gap = (column(stats_0, s * 4) - column(stats_1, s * 4)) * 0.5
        squares = column(stats_0, s * 4 + 1) + column(stats_1, s * 4 + 1)
        slope_0, slope_1, shift = [
            sums[s * 16 + i : s * 16 + i + 1]
            + sums[s * 16 + 3 + i : s * 16 + 4 + i]
            + sums[s * 16 + 6 + i : s * 16 + 7 + i]
            for i in range(3)
        ]
        inverse = lax.rsqrt(squares * (1.0 / D) + gap * gap + 1e-06)
        velocity = inverse * ((pay[s] + got_pay[s]) + gap * (slope_0 - slope_1)) + shift
        row_live = jnp.where(rows < heights[s], 1, 0)
        alive = m_id * 2 + l_id // 64 < widths[s] * row_live
        velocity = jnp.where(alive, velocity, 0.0)
        for m in range(16):
            vel_out[s, :, m * 128 : (m + 1) * 128] = velocity[m : m + 1]

    for copy in q_copies + l_copies + o_copies + a_copies + [b_copy, f_copy]:
        copy.wait_send()
    qs.close()
    ws.close()


def body(
    latents,
    heights,
    widths,
    slot_item,
    step_index,
    cond_table,
    text_kv,
    patch_weight,
    qkv_weight,
    out_weight,
    final_weight,
):
    constants = tables()
    vmem = pl.BlockSpec(memory_space=pltpu.VMEM)
    dma = pltpu.SemaphoreType.DMA
    shape = jax.ShapeDtypeStruct((2, 1, 2048), F32)
    velocity = pl.pallas_call(
        kernel,
        out_shape=shape,
        in_specs=[pl.BlockSpec(memory_space=pl.ANY)] * 18,
        out_specs=vmem,
        scratch_shapes=[
            pltpu.SMEM((2,), jnp.int32),
            pltpu.SMEM((2,), jnp.int32),
            pltpu.SMEM((2,), jnp.int32),
            pltpu.VMEM((2, 16, 128), F32),
            pltpu.VMEM((5, 16, D), F32),
            pltpu.VMEM((154, 2, 384), BF16),
            pltpu.VMEM((64, D), BF16),
            pltpu.VMEM((64, D), BF16),
            pltpu.VMEM((3, 6, 384), BF16),
            pltpu.VMEM((6, 384), BF16),
            pltpu.VMEM((1, D), jnp.int32),
            pltpu.VMEM((480, 1), jnp.int32),
            pltpu.VMEM((32, 1, D), F32),
            pltpu.VMEM((2, 16, D), F32),
            pltpu.VMEM((1, D // 2), jnp.int32),
            pltpu.VMEM((144, 1), jnp.int32),
            pltpu.VMEM((32, 1, D // 2), F32),
            pltpu.VMEM((2, 16, D // 2), F32),
            pltpu.VMEM((2, 16, 128), BF16),
            pltpu.VMEM((2, 32, 128), BF16),
            pltpu.VMEM((2, 16, 128), BF16),
            pltpu.VMEM((3, 32, 128), F32),
            pltpu.VMEM((32, 16, 128), BF16),
            pltpu.VMEM((16, 32, 128), BF16),
            pltpu.VMEM((32, 16, 128), BF16),
            pltpu.VMEM((16, UR, 640), BF16),
            pltpu.VMEM((16, UR // 2, 768), BF16),
            pltpu.VMEM((1024, D), BF16),
            pltpu.VMEM((1024, 384), BF16),
            pltpu.VMEM((2, 128, D), BF16),
            pltpu.VMEM((2, 128, D // 2), BF16),
            pltpu.VMEM((2, 128, D // 2), BF16),
            pltpu.VMEM((16, D), F32),
            pltpu.VMEM((16, D // 2), F32),
            pltpu.VMEM((48, D), F32),
            pltpu.VMEM((32, D), F32),
            pltpu.VMEM((176, D), BF16),
            pltpu.VMEM((112, D), F32),
            pltpu.VMEM((176, D // 2), F32),
            pltpu.VMEM((480, 512), BF16),
            pltpu.VMEM((144, 256), BF16),
            pltpu.VMEM((4, 32, 256), BF16),
            pltpu.VMEM((2, 4, 32, 256), BF16),
            pltpu.VMEM((3, 16, 128), F32),
            pltpu.VMEM((3, 16, 128), F32),
        ]
        + [dma((n,)) for n in (18, 16, 16, 16, 16, 32, 32, 8, 8, 8, 8, 8, 8, 8, 8, 8, 8, 1, 1, 1, 1)],
        compiler_params=pltpu.CompilerParams(
            collective_id=0, has_side_effects=True, vmem_limit_bytes=56 * 1024 * 1024
        ),
    )(
        heights,
        widths,
        slot_item,
        latents.reshape(2, 16, 128),
        cond_table.transpose(1, 0, 2),
        text_kv.transpose(0, 2, 1, 3),
        patch_weight,
        final_weight.T,
        qkv_weight,
        out_weight.T,
        *[jnp.asarray(constant) for constant in constants],
    )
    position = step_index[0].astype(F32)
    sigma_now = sigma_level(position)
    sigma_next = sigma_level(position + 1.0)
    return latents + (sigma_next - sigma_now) * velocity, latents - sigma_now * velocity


def solution(mesh):
    return jax.shard_map(
        body,
        mesh=mesh,
        in_specs=(
            P("item", "rows", None),
            P("item"),
            P("item"),
            P("item"),
            P(),
            P(),
            P("item", None, None, "hid"),
            P(),
            P(None, ("item", "rows"), "hid"),
            P("hid", ("item", "rows")),
            P(),
        ),
        out_specs=(P("item", "rows", None), P("item", "rows", None)),
        check_vma=False,
    )
```

```python
import functools

import jax
import jax.numpy as jnp
import numpy as np
from jax import lax
from jax.experimental import pallas as pl
from jax.experimental.pallas import tpu as pltpu
from jax.sharding import PartitionSpec as P

MESH = pl.DeviceIdType.MESH
HD = 64
STEPS = 28
D = 1536
NY, NZ = 8, 8
UR = 96
F32, BF16 = jnp.float32, jnp.bfloat16


def feature_order():
    order = np.zeros((D,), np.int32)
    at = 0
    for core in range(2):
        for outer in range(8):
            for inner in range(8):
                y, z = (outer, inner) if core == 0 else (inner, outer)
                for xh in range(2):
                    block = y * 32 + z * 4 + xh * 2 + core
                    order[at : at + 6] = 6 * block + np.arange(6)
                    at += 6
    return order


def tables():
    order = feature_order()
    quarter = D // 4
    frequency = (
        np.float32(1.0) / np.float32(10000.0) ** (np.arange(quarter, dtype=np.float32) / np.float32(quarter))
    ).astype(np.float32)
    angle = np.arange(32, dtype=np.float32)[:, None] * frequency[None, :]
    part = np.concatenate([np.sin(angle.astype(np.float64)), np.cos(angle.astype(np.float64))], 1)
    zero = np.zeros_like(part)
    row_table = np.concatenate([part, zero], 1)[:, order].astype(np.float32)
    col_table = np.concatenate([zero, part], 1)[:, order].astype(np.float32)
    pick = np.zeros((480, 1), np.int32)
    for tile in range(5):
        for source in range(16):
            for j in range(6):
                pick[tile * 96 + source * 6 + j, 0] = source * 32 + tile * 6 + j
    pick_out = np.zeros((144, 1), np.int32)
    for tile in range(3):
        for source in range(16):
            for j in range(3):
                pick_out[tile * 48 + source * 3 + j, 0] = source * 16 + tile * 3 + j
    col_table = np.stack([col_table[0::2], col_table[1::2]])
    place = np.arange(D).reshape(256, 2, 3)
    halves = np.stack([place[:, h].reshape(-1) for h in range(2)])
    return (
        order[None, :],
        pick,
        row_table[:, None, :],
        col_table,
        order[halves][:, None, :],
        pick_out,
        np.stack([row_table[:, None, half] for half in halves]),
        np.stack([col_table[:, :, half] for half in halves]),
    )


def sigma_level(position):
    fraction = 1.0 - position / STEPS
    return 3.0 * fraction / (1.0 + 2.0 * fraction)


def relative_partners():
    found = set()
    for dy in range(NY):
        for dz in range(NZ):
            for dxh in range(2):
                for dc in range(2):
                    for dxl in range(2):
                        near = (dy == 0 and dxl == 0 and dxh == 0) or (dy == 0 and dz == 0)
                        near = near or (dc == 0 and (dy == 0 or dz == 0))
                        if near:
                            found.add((dy, dz, dxh, dc, dxl))
    found.discard((0, 0, 0, 0, 0))
    return sorted(found)


def kernel(
    heights_in,
    widths_in,
    slot_in,
    lat_in,
    cond_in,
    text_in,
    wp_in,
    wft_in,
    wq_in,
    wo_in,
    order_in,
    pick_in,
    rowtab_in,
    coltab_in,
    order_h_in,
    pick_o_in,
    rowtab_h_in,
    coltab_h_in,
    vel_out,
    heights,
    widths,
    slot_item,
    lat,
    cond,
    text,
    wp,
    wft,
    wq,
    wo,
    order,
    pick,
    rowtab,
    coltab,
    order_h,
    pick_o,
    rowtab_h,
    coltab_h,
    latb,
    qpiece,
    opiece,
    piece,
    lb,
    qb,
    ob,
    qu,
    ou,
    nb,
    kvb,
    wps,
    wph,
    wfh,
    cperm,
    chalf,
    split,
    sums_in,
    rows_in,
    rows_out,
    rows_half,
    eb,
    eo,
    send_att,
    recv_att,
    pay,
    got_pay,
    sem_in,
    sem_ls,
    sem_lr,
    sem_qs,
    sem_qr,
    sem_os,
    sem_or,
    sem_us,
    sem_ur,
    sem_ps,
    sem_pr,
    sem_ws,
    sem_wr,
    sem_xs,
    sem_xr,
    sem_as,
    sem_ar,
    sem_bs,
    sem_br,
    sem_fs,
    sem_fr,
):
    y = lax.axis_index("item")
    rows = lax.axis_index("rows")
    xl = lax.axis_index("hid")
    z = rows // 4
    xh = (rows // 2) % 2
    core = rows % 2
    by_b = z * (1 - core) + y * core
    by_c = y * (1 - core) + z * core

    def flip(bit, change):
        return bit if change == 0 else 1 - bit

    def device(ty, tz, txh, tc, txl):
        return (ty, tz * 4 + txh * 2 + tc, txl)

    def ring_b(k):
        return (y + core * k) % 8, (z + (1 - core) * k) % 8

    def ring_c(k):
        return (y + (1 - core) * k) % 8, (z + core * k) % 8

    barrier = pltpu.get_barrier_semaphore()
    partners = relative_partners()
    for dy, dz, dxh, dc, dxl in partners:
        pl.semaphore_signal(
            barrier,
            inc=1,
            device_id=device((y + dy) % 8, (z + dz) % 8, flip(xh, dxh), flip(core, dc), flip(xl, dxl)),
            device_id_type=MESH,
        )
    pairs = (
        (wq_in, wq),
        (wo_in, wo),
        (lat_in, lat),
        (wp_in, wp),
        (wft_in, wft),
        (order_in, order),
        (pick_in, pick),
        (cond_in, cond),
        (rowtab_in, rowtab),
        (coltab_in, coltab),
        (text_in.at[core], text),
        (order_h_in.at[xl], order_h),
        (pick_o_in, pick_o),
        (rowtab_h_in.at[xl], rowtab_h),
        (coltab_h_in.at[xl], coltab_h),
        (heights_in, heights),
        (widths_in, widths),
        (slot_in, slot_item),
    )
    loads = [pltpu.make_async_copy(a, b, sem_in.at[i]) for i, (a, b) in enumerate(pairs)]
    for load in loads:
        load.start()
    loads[0].wait()
    for q in range(2):
        cut = slice(q * 192, (q + 1) * 192)
        parts = [wq[i].astype(F32)[:, cut] for i in (1, 2, 0)]
        full = jnp.concatenate(parts + [jnp.zeros((6, 64), F32)], 1)
        for t in range(5):
            piece[q, t * 6 : t * 6 + 6] = full[:, t * 128 : (t + 1) * 128]
        piece[q, 30:32] = jnp.zeros((2, 128), F32)
        qpiece[q] = piece[q].astype(BF16)
    loads[1].wait()
    for half in range(2):
        for t in range(3):
            at = half * 16 + t * 3
            piece[2, at : at + 3] = wo[...].astype(F32)[half * 3 : half * 3 + 3, t * 128 : (t + 1) * 128]
        piece[2, half * 16 + 9 : half * 16 + 16] = jnp.zeros((7, 128), F32)
        opiece[half] = piece[2, half * 16 : half * 16 + 16].astype(BF16)
    loads[2].wait()
    latb[...] = lat[...].astype(BF16)
    my_lat = xh * 16 + z * 2 + core
    lb[my_lat] = latb[core]
    qb[by_b * 2 + xh] = qpiece[xh]
    ob[xl * 16 + by_b * 2 + xh] = opiece[xl]
    pl.semaphore_wait(barrier, len(partners))

    def remote(src, dst, s_sem, r_sem, to):
        return pltpu.make_async_remote_copy(
            src_ref=src, dst_ref=dst, send_sem=s_sem, recv_sem=r_sem, device_id=to, device_id_type=MESH
        )

    q_copies, l_copies, o_copies = [], [], []
    for k in range(8):
        for dxh in range(2):
            if k == 0 and dxh == 0:
                continue
            ty, tz = ring_b(k)
            txh = flip(xh, dxh)
            n = k * 2 + dxh
            q_copies.append(
                remote(
                    qpiece.at[txh],
                    qb.at[by_b * 2 + xh],
                    sem_qs.at[n],
                    sem_qr.at[n],
                    device(ty, tz, txh, core, xl),
                )
            )
            q_copies[-1].start()
    for dz in range(8):
        for dc in range(2):
            n = dz * 2 + dc
            if n == 0:
                continue
            tc = flip(core, dc)
            l_copies.append(
                remote(
                    latb.at[tc],
                    lb.at[my_lat],
                    sem_ls.at[n],
                    sem_lr.at[n],
                    device(y, (z + dz) % 8, xh, tc, xl),
                )
            )
            l_copies[-1].start()
    for k in range(8):
        for dxh in range(2):
            for dxl in range(2):
                n = k * 4 + dxh * 2 + dxl
                if n == 0:
                    continue
                ty, tz = ring_b(k)
                o_copies.append(
                    remote(
                        opiece.at[flip(xl, dxl)],
                        ob.at[xl * 16 + by_b * 2 + xh],
                        sem_os.at[n],
                        sem_or.at[n],
                        device(ty, tz, flip(xh, dxh), core, flip(xl, dxl)),
                    )
                )
                o_copies[-1].start()


    for load in loads[3:]:
        load.wait()
    eb[...] = (lax.broadcasted_iota(jnp.int32, (480, 512), 1) == pick[...]).astype(F32).astype(BF16)
    eo[...] = (lax.broadcasted_iota(jnp.int32, (144, 256), 1) == pick_o[...]).astype(F32).astype(BF16)

    for copy in q_copies:
        copy.wait_recv()
    packed = jnp.dot(eb[...], qb[...].reshape(512, 128), preferred_element_type=F32).astype(BF16)
    mine = core * 8 + by_c
    for t in range(5):
        qu[mine, :, t * 128 : (t + 1) * 128] = packed[t * 96 : (t + 1) * 96]

    def unit(step):
        return core * 8 + (by_c + step + 8) % 8

    class Spread:
        def __init__(self, buf, s_sem, r_sem, ps_sem, pr_sem):
            self.buf, self.s, self.r, self.ps, self.pr = buf, s_sem, r_sem, ps_sem, pr_sem
            self.cut = buf.shape[1] // 32 * 16 + buf.shape[1] % 32
            self.sent, self.come = [], {}
            self.partner = []

        def send(self, n, origin, step, part=slice(None)):
            ty, tz = ring_c((step + 8) % 8)
            block = self.buf.at[unit(origin), part]
            c = remote(
                block,
                block,
                self.s.at[n],
                self.r.at[n],
                device(ty, tz, xh, core, xl),
            )
            c.start()
            self.sent.append(c)
            self.come[n] = c

        def share(self, n, origin):
            slot = unit(origin)
            c = remote(
                self.buf.at[slot],
                self.buf.at[slot],
                self.ps.at[n],
                self.pr.at[n],
                device(y, z, xh, 1 - core, xl),
            )
            c.start()
            self.partner.append(c)

        def first(self):
            self.send(0, 0, 2)
            self.send(1, 0, -2)
            self.send(2, 0, 1)
            self.send(3, 0, -1)
            self.share(0, 0)

        def second(self):
            self.come[0].wait_recv()
            self.send(6, -2, 2, slice(0, self.cut))
            self.send(4, -2, 1)
            self.come[1].wait_recv()
            self.send(7, 2, -2, slice(self.cut, None))
            self.send(5, 2, -1)
            self.share(1, -2)
            self.share(2, 2)
            self.come[2].wait_recv()
            self.share(3, -1)
            self.come[3].wait_recv()
            self.share(4, 1)

        def third(self):
            self.come[4].wait_recv()
            self.share(5, -3)
            self.come[5].wait_recv()
            self.share(6, 3)
            self.come[6].wait_recv()
            self.come[7].wait_recv()
            self.share(7, -4)

        def last(self):
            for c in self.partner:
                c.wait_recv()

        def close(self):
            for c in self.sent + self.partner:
                c.wait_send()

    qs = Spread(qu, sem_us, sem_ur, sem_ps, sem_pr)
    qs.first()
    for copy in l_copies:
        copy.wait_recv()
    block = lb.at[pl.ds(pl.multiple_of(xh * 16, 16), 16)]
    b_copy = remote(block, block, sem_bs.at[0], sem_br.at[0], device(y, z, 1 - xh, core, xl))
    b_copy.start()

    rows_in[0:64] = wp[...]
    rows_in[112:176] = wft[...]

    def three(value):
        hi = value.astype(BF16).astype(F32)
        mid = (value - hi).astype(BF16).astype(F32)
        return hi, mid, (value - hi - mid).astype(BF16).astype(F32)

    in_first = (lax.broadcasted_iota(jnp.int32, (1, D), 1) % 6) < 3
    for s in range(2):
        c = jnp.concatenate([cond[i, pl.ds(slot_item[s], 1)] for i in range(5)], 0)
        for i, part in enumerate(three(c)):
            at = s * 24 + i * 8
            split[at : at + 8] = jnp.concatenate([part, jnp.zeros((3, D), F32)], 0)
        scale_f = 1.0 + c[4:5]
        first = jnp.where(in_first, scale_f, 0.0)
        three_rows = jnp.concatenate([first, scale_f - first, c[3:4]], 0)
        parts = three(three_rows)
        sums_in[s * 16 : s * 16 + 16] = jnp.concatenate(list(parts) + [jnp.zeros((7, D), F32)], 0)
    rows_in[64:112] = split[...].astype(BF16)

    def onehot(names):
        return (lax.broadcasted_iota(jnp.int32, (D, 256), 0) == names).astype(F32).astype(BF16)

    for i in range(6):
        cols = slice(i * 256, (i + 1) * 256)
        rows_out[:, cols] = jnp.dot(rows_in[0:112], onehot(order[:, cols]), preferred_element_type=F32)
    for i in range(3):
        cols = slice(i * 256, (i + 1) * 256)
        rows_half[:, cols] = jnp.dot(rows_in[...], onehot(order_h[:, cols]), preferred_element_type=F32)
    for at, rest in ((0, 64), (1, 0)):
        wps[at, at * 64 : at * 64 + 64] = rows_out[0:64].astype(BF16)
        wps[at, rest : rest + 64] = jnp.zeros((64, D), BF16)
        wph[at, at * 64 : at * 64 + 64] = rows_half[0:64].astype(BF16)
        wph[at, rest : rest + 64] = jnp.zeros((64, D // 2), BF16)
        wfh[at, at * 64 : at * 64 + 64] = rows_half[112:176].astype(BF16)
        wfh[at, rest : rest + 64] = jnp.zeros((64, D // 2), BF16)
    for s in range(2):
        at = 64 + s * 24
        for src, dst in ((rows_out, cperm), (rows_half, chalf)):
            dst[s * 8 : s * 8 + 8] = src[at : at + 8] + src[at + 8 : at + 16] + src[at + 16 : at + 24]
    nt = (((1,), (1,)), ((), ()))
    final_rows = jnp.concatenate([wft[...], wft[...]], 0)
    sums = lax.dot_general(sums_in[...].astype(BF16), final_rows, nt, preferred_element_type=F32)

    r_id = lax.broadcasted_iota(jnp.int32, (384, 384), 0)
    c_id = lax.broadcasted_iota(jnp.int32, (384, 384), 1)
    pick_key = ((r_id == c_id + 192 * xh) & (c_id < 192)).astype(F32).astype(BF16)
    pick_val = ((r_id == c_id - 192 + 192 * xh) & (c_id >= 192)).astype(F32).astype(BF16)
    place = [
        ((r_id - 64 + 192 * g == c_id) & (r_id >= 64)).astype(F32).astype(BF16)[0:256] for g in range(2)
    ]
    text_rows = (
        jnp.dot(text[:, 0], pick_key, preferred_element_type=F32)
        + jnp.dot(text[:, 1], pick_val, preferred_element_type=F32)
    ).astype(BF16)

    def normalise(value):
        mean = jnp.mean(value, -1, keepdims=True)
        centered = value - mean
        return centered * lax.rsqrt(jnp.mean(centered * centered, -1, keepdims=True) + 1e-06)

    cmine = cperm[pl.ds(pl.multiple_of(core * 8, 8), 8)]
    shift_a, scale_a = cmine[0:1], 1.0 + cmine[1:2]

    def norm_half(half):
        def chunk(i, carry):
            x = lb[pl.ds(half * 16 + i * 4, 4)].reshape(64, 128)
            for parity in range(2):
                e = jnp.dot(x, wps[parity], preferred_element_type=F32)
                for rr in range(4):
                    row = (i * 2 + rr // 2) * 4 + half * 2 + rr % 2
                    part = e[rr * 16 : rr * 16 + 16] + (rowtab[row] + coltab[parity])
                    at = (row // 4) * 128 + parity * 64 + (row % 4) * 16
                    nb[pl.ds(pl.multiple_of(at, 16), 16)] = (normalise(part) * scale_a + shift_a).astype(BF16)
            return carry

        lax.fori_loop(0, 4, chunk, 0)

    norm_half(xh)
    qs.second()
    for copy in o_copies:
        copy.wait_recv()
    for half in range(2):
        got = jnp.dot(
            eo[...], ob[half * 16 : half * 16 + 16].reshape(256, 128), preferred_element_type=F32
        ).astype(BF16)
        for t in range(3):
            ou[mine, :, half * 384 + t * 128 : half * 384 + (t + 1) * 128] = got[t * 48 : (t + 1) * 48]
    ws = Spread(ou, sem_ws, sem_wr, sem_xs, sem_xr)
    ws.first()
    b_copy.wait_recv()
    norm_half(1 - xh)
    qs.third()
    qs.last()

    kvb[...] = jnp.dot(nb[...], qu[:, :, 0:384].reshape(D, 384), preferred_element_type=F32).astype(BF16)
    queries = jnp.dot(
        nb[pl.ds(pl.multiple_of(z * 128, 128), 128)],
        qu[:, :, 384:640].reshape(D, 256),
        preferred_element_type=F32,
    ).astype(BF16)
    ws.second()

    height, width = heights[core], widths[core]
    key_id = lax.broadcasted_iota(jnp.int32, (1, 1024), 1)
    key_row = (key_id // 128) * 4 + (key_id // 16) % 4
    key_col = (key_id % 16) * 2 + (key_id // 64) % 2
    live = (key_row < height) & (key_col < width)
    lane = lax.broadcasted_iota(jnp.int32, (1, 256), 1)
    keys, values = kvb[:, 0:256], kvb[:, 128:384]
    attended = jnp.zeros((128, 256), F32)
    masked = [
        jnp.where((lane >= 64 * h) & (lane < 64 * h + 64), queries.astype(F32) * HD ** (-0.5), 0.0).astype(BF16) for h in range(3)
    ]
    stacked = jnp.concatenate(masked, 0)
    s_text = lax.dot_general(stacked, text_rows[:, 0:256], nt, preferred_element_type=F32)
    s_img = lax.dot_general(stacked, keys, nt, preferred_element_type=F32)
    s_img = jnp.where(live, s_img, -1e30)
    top = jnp.maximum(jnp.max(s_text, -1, keepdims=True), jnp.max(s_img, -1, keepdims=True))
    w_text = jnp.exp(s_text - top)
    w_img = jnp.exp(s_img - top)
    total = jnp.sum(w_text, -1, keepdims=True) + jnp.sum(w_img, -1, keepdims=True)
    acc = jnp.dot(w_text.astype(BF16), text_rows[:, 128:384], preferred_element_type=F32) + jnp.dot(
        w_img.astype(BF16), values, preferred_element_type=F32
    )
    acc = acc * (1.0 / total)
    for h in range(3):
        inside = (lane >= 64 + 64 * h) & (lane < 128 + 64 * h)
        attended = attended + jnp.where(inside, acc[h * 128 : (h + 1) * 128], 0.0)
    placed = attended.astype(BF16)
    for j in range(4):
        for parity in range(2):
            send_att[j, parity * 16 : parity * 16 + 16] = placed[
                parity * 64 + j * 16 : parity * 64 + j * 16 + 16
            ]
    head_at = xl * 2 + xh
    a_copies = []
    for n in range(1, 8):
        txh, tc, txl = flip(xh, n // 4), flip(core, (n // 2) % 2), flip(xl, n % 2)
        a_copies.append(
            remote(
                send_att.at[txh * 2 + tc],
                recv_att.at[core, head_at],
                sem_as.at[n],
                sem_ar.at[n],
                device(y, z, txh, tc, txl),
            )
        )
        a_copies[-1].start()
    recv_att[core, head_at] = send_att[xh * 2 + core]
    ws.third()
    ws.last()
    for copy in a_copies:
        copy.wait_recv()

    halves = []
    for g in range(2):
        sides = [jnp.concatenate([recv_att[s, 2 * g + side] for s in range(2)], 0) for side in range(2)]
        halves.append(
            (
                jnp.dot(sides[0], place[0], preferred_element_type=F32)
                + jnp.dot(sides[1], place[1], preferred_element_type=F32)
            ).astype(BF16)
        )
    projected = lax.dot_general(
        jnp.concatenate(halves, 1), ou[...].reshape(D // 2, 768), nt, preferred_element_type=F32
    )
    l_id = lax.broadcasted_iota(jnp.int32, (16, 128), 1)
    stats = jnp.zeros((16, 128), F32)
    for s in range(2):
        gate = chalf[s * 8 + 2 : s * 8 + 3]
        scale_f = 1.0 + chalf[s * 8 + 4 : s * 8 + 5]
        product = jnp.zeros((16, 128), F32)
        for parity in range(2):
            e = jnp.dot(latb[s], wph[parity], preferred_element_type=F32) + (rowtab_h[rows] + coltab_h[parity])
            at = s * 32 + parity * 16
            residual = e + gate * projected[at : at + 16]
            mean = jnp.mean(residual, -1, keepdims=True)
            centered = residual - mean
            squares = jnp.sum(centered * centered, -1, keepdims=True)
            stats = jnp.where(l_id == s * 4 + parity * 2, mean, stats)
            stats = jnp.where(l_id == s * 4 + parity * 2 + 1, squares, stats)
            product = product + lax.dot_general(
                (centered * scale_f).astype(BF16), wfh[parity], nt, preferred_element_type=F32
            )
        pay[s] = product
    pay[2] = stats
    f_copy = remote(pay, got_pay, sem_fs.at[0], sem_fr.at[0], device(y, z, xh, core, 1 - xl))
    f_copy.start()
    f_copy.wait_recv()
    stats_0 = jnp.where(xl == 0, pay[2], got_pay[2])
    stats_1 = jnp.where(xl == 0, got_pay[2], pay[2])

    def column(tile, at):
        even, odd = [jnp.sum(jnp.where(l_id == at + p, tile, 0.0), -1, keepdims=True) for p in (0, 2)]
        return jnp.where(l_id < 64, even, odd)

    m_id = lax.broadcasted_iota(jnp.int32, (16, 128), 0)
    for s in range(2):
        gap = (column(stats_0, s * 4) - column(stats_1, s * 4)) * 0.5
        squares = column(stats_0, s * 4 + 1) + column(stats_1, s * 4 + 1)
        slope_0, slope_1, shift = [
            sums[s * 16 + i : s * 16 + i + 1]
            + sums[s * 16 + 3 + i : s * 16 + 4 + i]
            + sums[s * 16 + 6 + i : s * 16 + 7 + i]
            for i in range(3)
        ]
        inverse = lax.rsqrt(squares * (1.0 / D) + gap * gap + 1e-06)
        velocity = inverse * ((pay[s] + got_pay[s]) + gap * (slope_0 - slope_1)) + shift
        row_live = jnp.where(rows < heights[s], 1, 0)
        alive = m_id * 2 + l_id // 64 < widths[s] * row_live
        velocity = jnp.where(alive, velocity, 0.0)
        for m in range(16):
            vel_out[s, :, m * 128 : (m + 1) * 128] = velocity[m : m + 1]

    for copy in q_copies + l_copies + o_copies + a_copies + [b_copy, f_copy]:
        copy.wait_send()
    qs.close()
    ws.close()


def body(
    latents,
    heights,
    widths,
    slot_item,
    step_index,
    cond_table,
    text_kv,
    patch_weight,
    qkv_weight,
    out_weight,
    final_weight,
):
    constants = tables()
    vmem = pl.BlockSpec(memory_space=pltpu.VMEM)
    dma = pltpu.SemaphoreType.DMA
    shape = jax.ShapeDtypeStruct((2, 1, 2048), F32)
    velocity = pl.pallas_call(
        kernel,
        out_shape=shape,
        in_specs=[pl.BlockSpec(memory_space=pl.ANY)] * 18,
        out_specs=vmem,
        scratch_shapes=[
            pltpu.SMEM((2,), jnp.int32),
            pltpu.SMEM((2,), jnp.int32),
            pltpu.SMEM((2,), jnp.int32),
            pltpu.VMEM((2, 16, 128), F32),
            pltpu.VMEM((5, 16, D), F32),
            pltpu.VMEM((154, 2, 384), BF16),
            pltpu.VMEM((64, D), BF16),
            pltpu.VMEM((64, D), BF16),
            pltpu.VMEM((3, 6, 384), BF16),
            pltpu.VMEM((6, 384), BF16),
            pltpu.VMEM((1, D), jnp.int32),
            pltpu.VMEM((480, 1), jnp.int32),
            pltpu.VMEM((32, 1, D), F32),
            pltpu.VMEM((2, 16, D), F32),
            pltpu.VMEM((1, D // 2), jnp.int32),
            pltpu.VMEM((144, 1), jnp.int32),
            pltpu.VMEM((32, 1, D // 2), F32),
            pltpu.VMEM((2, 16, D // 2), F32),
            pltpu.VMEM((2, 16, 128), BF16),
            pltpu.VMEM((2, 32, 128), BF16),
            pltpu.VMEM((2, 16, 128), BF16),
            pltpu.VMEM((3, 32, 128), F32),
            pltpu.VMEM((32, 16, 128), BF16),
            pltpu.VMEM((16, 32, 128), BF16),
            pltpu.VMEM((32, 16, 128), BF16),
            pltpu.VMEM((16, UR, 640), BF16),
            pltpu.VMEM((16, UR // 2, 768), BF16),
            pltpu.VMEM((1024, D), BF16),
            pltpu.VMEM((1024, 384), BF16),
            pltpu.VMEM((2, 128, D), BF16),
            pltpu.VMEM((2, 128, D // 2), BF16),
            pltpu.VMEM((2, 128, D // 2), BF16),
            pltpu.VMEM((16, D), F32),
            pltpu.VMEM((16, D // 2), F32),
            pltpu.VMEM((48, D), F32),
            pltpu.VMEM((32, D), F32),
            pltpu.VMEM((176, D), BF16),
            pltpu.VMEM((112, D), F32),
            pltpu.VMEM((176, D // 2), F32),
            pltpu.VMEM((480, 512), BF16),
            pltpu.VMEM((144, 256), BF16),
            pltpu.VMEM((4, 32, 256), BF16),
            pltpu.VMEM((2, 4, 32, 256), BF16),
            pltpu.VMEM((3, 16, 128), F32),
            pltpu.VMEM((3, 16, 128), F32),
        ]
        + [dma((n,)) for n in (18, 16, 16, 16, 16, 32, 32, 8, 8, 8, 8, 8, 8, 8, 8, 8, 8, 1, 1, 1, 1)],
        compiler_params=pltpu.CompilerParams(
            collective_id=0, has_side_effects=True, vmem_limit_bytes=56 * 1024 * 1024
        ),
    )(
        heights,
        widths,
        slot_item,
        latents.reshape(2, 16, 128),
        cond_table.transpose(1, 0, 2),
        text_kv.transpose(0, 2, 1, 3),
        patch_weight,
        final_weight.T,
        qkv_weight,
        out_weight.T,
        *[jnp.asarray(constant) for constant in constants],
    )
    position = step_index[0].astype(F32)
    sigma_now = sigma_level(position)
    sigma_next = sigma_level(position + 1.0)
    return latents + (sigma_next - sigma_now) * velocity, latents - sigma_now * velocity


def solution(mesh):
    return jax.shard_map(
        body,
        mesh=mesh,
        in_specs=(
            P("item", "rows", None),
            P("item"),
            P("item"),
            P("item"),
            P(),
            P(),
            P("item", None, None, "hid"),
            P(),
            P(None, ("item", "rows"), "hid"),
            P("hid", ("item", "rows")),
            P(),
        ),
        out_specs=(P("item", "rows", None), P("item", "rows", None)),
        check_vma=False,
    )
```
